128 devices in a mesh: view: 8 (over y_hi, x), gz: 16 (over z, y_lo, core).
Axes of the slice: x: 4, y: 4 (y_hi: 2, y_lo: 2; y = y_hi * 2 + y_lo), z: 4, core: 2. Of those that a mesh axis runs over, the one named last changes fastest.
Arguments:
- views_data: float32 [8, 256, 96, 1024], P('view', 'gz'), may hold values from 0.2 to 40
- estimate: float32 [256, 96, 1024], P('gz'), may hold values from 0.5 to 1.5
- kernels: float32 [8, 3, 31], P('view'), may hold values from 0.001 to 3
Outputs:
- deconvolved: float32 [256, 96, 1024], P('gz')
The draws below stay inside these ranges and needn't reach their ends.
All inputs are finite; a program needn't handle non-finite values.
Results may differ from the reference program's by a relative error of at most 0.0001.
Values sent between devices are 32-bit elements; how exact they have to be, the bound alone decides.
No kernel may reach another device: no remote copies, remote signals or barrier semaphores. Data moves between devices by JAX's collectives and lax.ppermute only.
A program may use at most 128 MiB of HBM per device.

```python
import jax
import jax.numpy as jnp
from jax import lax

X = 1024
Y = 96
TAPS = 31
ITERS = 2
RADIUS = 15
VIEWS = 8
Z = 256


def draw_kernels(key, part):
    streams = jax.random.split(key, 5)
    offsets = (jnp.arange(TAPS) - RADIUS).astype(jnp.float32)
    lateral_sigma = jax.random.uniform(streams[0], (VIEWS, 2, 1), jnp.float32, 1.0, 2.0)
    lateral_scaled = offsets / lateral_sigma
    lateral = jnp.exp(-0.5 * lateral_scaled * lateral_scaled) + 0.002
    axial_sigma = jax.random.uniform(streams[1], (VIEWS, 1, 1), jnp.float32, 2.0, 4.0)
    axial_width = jax.random.uniform(streams[2], (VIEWS, 1, 1), jnp.float32, 3.0, 6.0)
    axial_weight = jax.random.uniform(streams[3], (VIEWS, 1, 1), jnp.float32, 0.3, 1.0)
    core_scaled = offsets / axial_sigma
    tail_scaled = offsets / axial_width
    axial = jnp.exp(-0.5 * core_scaled * core_scaled) + axial_weight / (1.0 + tail_scaled * tail_scaled)
    jitter = jax.random.uniform(streams[4], (VIEWS, 3, TAPS), jnp.float32, 0.8, 1.2)
    return jnp.concatenate([lateral, axial], axis=1) * jitter


def draw_views_data(key, part):
    streams = jax.random.split(key, 5)
    points = (jax.random.randint(streams[0], (Z, Y, X), 0, 16) == 0).astype(jnp.float32)
    bright = jax.random.uniform(streams[1], (Z, Y, X), jnp.float32, 2.0, 8.0)
    sample = 1.0 + points * bright
    loudness = jax.random.uniform(streams[3], (VIEWS, 1, 1, 1), jnp.float32, 0.6, 1.6)
    jitter = jax.random.uniform(streams[4], (VIEWS, Z, Y, X), jnp.float32, 0.75, 1.25)
    return loudness * sample[None] * jitter


def steps_of(rng, extent, cuts, smallest, largest):
    factor_of = 1.0
    for position, parts in cuts:
        steps = jax.random.uniform(jax.random.fold_in(jax.random.fold_in(rng, 6), position), (parts,), jnp.float32, smallest / len(cuts), largest / len(cuts))
        factor_of = factor_of * jnp.repeat(jnp.exp(steps), extent[position] // parts).reshape((-1,) + (1,) * (len(extent) - 1 - position))
    return factor_of


def setup_inputs(seed: int = 0) -> dict:
    arg_keys = jax.random.split(jax.random.key(seed), 4)
    views_data = draw_views_data(jax.random.fold_in(arg_keys[3], 71), 0)
    estimate = jnp.clip(0.5 + 1.0 * jax.random.uniform(arg_keys[1], (Z, Y, X), jnp.float32) ** steps_of(arg_keys[1], (Z, Y, X), ((0, 16),), -0.2, 0.2), 0.5, 1.5)
    kernels = draw_kernels(jax.random.fold_in(arg_keys[3], 71), 0)
    return dict(views_data=views_data, estimate=estimate, kernels=kernels)


def toeplitz(tap_values, count):
    row_pos = jnp.arange(count)[:, None]
    col_pos = jnp.arange(count)[None, :]
    offsets = row_pos - col_pos + RADIUS
    matrix = jnp.zeros((count, count), jnp.float32)
    for offset in range(TAPS):
        matrix = matrix + jnp.where(offsets == offset, tap_values[offset], 0.0)
    return matrix


def z_filter(volume, tap_values, flipped):
    depth = volume.shape[0]
    padded = jnp.pad(volume, ((RADIUS, RADIUS), (0, 0), (0, 0)))
    result = jnp.zeros_like(volume)
    for offset in range(TAPS):
        start = 2 * RADIUS - offset if flipped else offset
        result = result + tap_values[offset] * padded[start:start + depth]
    return result


def blur(volume, kernel_set, flipped):
    mat_x = toeplitz(kernel_set[0], volume.shape[2])
    mat_y = toeplitz(kernel_set[1], volume.shape[1])
    if flipped:
        mat_x = mat_x.T
        mat_y = mat_y.T
    passed = jnp.dot(volume, mat_x, precision=lax.Precision.HIGHEST)
    passed = jnp.einsum("zyx,yw->zwx", passed, mat_y, precision=lax.Precision.HIGHEST)
    return z_filter(passed, kernel_set[2], flipped)


def reference(views_data, estimate, kernels):
    tap_norm = kernels / jnp.sum(kernels, axis=-1, keepdims=True)
    for number in range(ITERS):
        logsum = jnp.zeros_like(estimate)
        for view_number in range(VIEWS):
            blurred = blur(estimate, tap_norm[view_number], False)
            ratio = views_data[view_number] / blurred
            back = blur(ratio, tap_norm[view_number], True)
            logsum = logsum + jnp.log(back)
        estimate = estimate * jnp.exp(logsum / VIEWS)
    return estimate
```

```python
import jax
import jax.numpy as jnp
from jax import lax
from jax.experimental import pallas as pl
from jax.experimental.pallas import tpu as pltpu
from jax.sharding import Mesh
from jax.sharding import PartitionSpec as P

TAPS = 31
ITERS = 2
RADIUS = 15
HALO = 16
VIEWS = 8
ZC = 64
YC = 24
XC = 128
YW = 64
ZW = ZC + 2 * HALO
SLABS = 4
V = ("yh", "x")
S = ("yl", "co")
F32 = jnp.float32
BF16 = jnp.bfloat16
LIMIT = 58 * 1024 * 1024


def split(value):
    hi = value.astype(BF16)
    return hi, (value - hi.astype(F32)).astype(BF16)


def split_constant(value):
    hi = lax.reduce_precision(value, 8, 7)
    return hi.astype(BF16), (value - hi).astype(BF16)


def dot(a, b):
    return jnp.dot(a, b, preferred_element_type=F32)


def banded(taps, offsets):
    result = jnp.zeros((taps.shape[0],) + offsets.shape, F32)
    for t in range(TAPS):
        result = result + jnp.where(offsets == t, taps[:, t, None, None], 0.0)
    return result


def neighbours(axis, size):
    up = [(i, i + 1) for i in range(size - 1)]
    return up, [(j, i) for i, j in up]


def exchange(low, high, axis, size):
    up, down = neighbours(axis, size)
    return lax.ppermute(high, axis, up), lax.ppermute(low, axis, down)


def z_sum(win, taps, v, store):
    @pl.loop(0, ZC // 16)
    def _(b):
        z0 = pl.multiple_of(b * 16, 16)
        for y0 in range(0, YC, 8):
            acc = jnp.zeros((16, 8, XC), F32)
            for t in range(TAPS):
                acc = acc + taps[v, t] * win[pl.ds(z0 + t + 1, 16), y0 : y0 + 8, :]
            store(z0, y0, acc)


def forward_kernel(taps, est, data, wy, wxa, wxb, ratio, left, right, yhi, ylo, win):
    v = pl.program_id(0)

    @pl.when(v == 0)
    def _():
        @pl.loop(0, ZW // 2)
        def _(b):
            both = []
            for k in range(2):
                hi, lo = split(est[2 * b + k])
                stacked = jnp.concatenate([hi, lo, hi], axis=0)
                both.append(dot(wy[...], stacked))
            rows = pl.ds(pl.multiple_of(b * 2 * YC, 16), 2 * YC)
            for u in range(VIEWS):
                pair = jnp.concatenate([o[u * YC : (u + 1) * YC] for o in both], axis=0)
                hi, lo = split(pair)
                yhi[u, rows, :] = hi
                ylo[u, rows, :] = lo

    planes = 16

    @pl.loop(0, ZW // planes)
    def _(b):
        rows = pl.ds(pl.multiple_of(b * planes * YC, 16), planes * YC)
        two = dot(yhi[v, rows, :], wxa[0])
        out = two[:, :XC] + two[:, XC:] + dot(ylo[v, rows, :], wxb[0])
        win[pl.ds(pl.multiple_of(b * planes, planes), planes)] = out.reshape(planes, YC, XC)

    mine = lax.broadcasted_iota(jnp.int32, (16, 8, XC), 2) // HALO == v

    def store(z0, y0, blurred):
        zs = pl.ds(z0, 16)
        value = data[0, zs, y0 : y0 + 8, :] / blurred
        ratio[0, zs, y0 : y0 + 8, :] = value
        first = pltpu.roll(value, HALO * v, 2)
        last = pltpu.roll(value, lax.rem(HALO * v + HALO, XC), 2)
        left[zs, y0 : y0 + 8, :] = jnp.where(mine, first, left[zs, y0 : y0 + 8, :])
        right[zs, y0 : y0 + 8, :] = jnp.where(mine, last, right[zs, y0 : y0 + 8, :])

    z_sum(win, taps, v, store)


def forward(tz, window, data, wy, wxa, wxb):
    one = pl.Buffered(1)
    view = pl.BlockSpec((1, ZC, YC, XC), lambda v: (v, 0, 0, 0))
    pack = pl.BlockSpec((ZC, YC, XC), lambda v: (0, 0, 0))
    shape = jax.ShapeDtypeStruct((ZC, YC, XC), F32)
    return pl.pallas_call(
        forward_kernel,
        name="forward",
        grid=(VIEWS,),
        out_shape=(jax.ShapeDtypeStruct((VIEWS, ZC, YC, XC), F32), shape, shape),
        in_specs=[
            pl.BlockSpec(memory_space=pltpu.SMEM),
            pl.BlockSpec((ZW, YW, 2 * XC), lambda v: (0, 0, 0), pipeline_mode=one),
            view,
            pl.BlockSpec((VIEWS * YC, 3 * YW), lambda v: (0, 0), pipeline_mode=one),
            pl.BlockSpec((1, 2 * XC, 2 * XC), lambda v: (v, 0, 0)),
            pl.BlockSpec((1, 2 * XC, XC), lambda v: (v, 0, 0)),
        ],
        out_specs=(view, pack, pack),
        scratch_shapes=[
            pltpu.VMEM((VIEWS, ZW * YC, 2 * XC), BF16),
            pltpu.VMEM((VIEWS, ZW * YC, 2 * XC), BF16),
            pltpu.VMEM((ZW, YC, XC), F32),
        ],
        compiler_params=pltpu.CompilerParams(vmem_limit_bytes=LIMIT),
    )(tz, window, data, wy, wxa, wxb)


def adjoint_x_kernel(ratio, before, after, wown, wha, whb, out, top, bottom):
    planes = 16

    @pl.loop(0, ZC // planes)
    def _(b):
        zs = pl.ds(pl.multiple_of(b * planes, planes), planes)
        rows = planes * YC
        hi, lo = split(ratio[0, zs].reshape(rows, XC))
        sides = jnp.concatenate([before[zs].reshape(rows, XC), after[zs].reshape(rows, XC)], axis=1)
        shi, slo = split(sides)
        two = dot(jnp.concatenate([hi, lo], axis=1), wown[0]) + dot(shi, wha[0])
        value = two[:, :XC] + two[:, XC:] + dot(slo, whb[0])
        value = value.reshape(planes, YC, XC)
        out[0, zs] = value
        top[0, zs] = value[:, :HALO]
        bottom[0, zs] = value[:, YC - HALO :]


def adjoint_x(ratio, before, after, wown, wha, whb):
    views = ratio.shape[0]
    view = pl.BlockSpec((1, ZC, YC, XC), lambda v: (v, 0, 0, 0))
    pack = pl.BlockSpec((ZC, YC, XC), lambda v: (0, 0, 0))
    edge = pl.BlockSpec((1, ZC, HALO, XC), lambda v: (v, 0, 0, 0))
    edge_shape = jax.ShapeDtypeStruct((views, ZC, HALO, XC), F32)
    return pl.pallas_call(
        adjoint_x_kernel,
        name="adjoint_x",
        grid=(views,),
        out_shape=(jax.ShapeDtypeStruct((views, ZC, YC, XC), F32), edge_shape, edge_shape),
        in_specs=[
            view,
            pack,
            pack,
            pl.BlockSpec((1, 2 * XC, 2 * XC), lambda v: (v, 0, 0)),
            pl.BlockSpec((1, 2 * XC, 2 * XC), lambda v: (v, 0, 0)),
            pl.BlockSpec((1, 2 * XC, XC), lambda v: (v, 0, 0)),
        ],
        out_specs=(view, edge, edge),
        compiler_params=pltpu.CompilerParams(vmem_limit_bytes=LIMIT),
    )(ratio, before, after, wown, wha, whb)


def adjoint_y_kernel(value, before, after, wy, out, low, high):
    empty = jnp.zeros((YW - YC - 2 * HALO, 2 * XC), F32)

    def pair(ref, z):
        return jnp.concatenate([ref[0, z], ref[0, z + 1]], axis=1)

    @pl.loop(0, ZC // 2, unroll=4)
    def _(b):
        z = 2 * b
        rows = jnp.concatenate([pair(before, z), pair(value, z), pair(after, z), empty], axis=0)
        hi, lo = split(rows)
        got = dot(wy[0], jnp.concatenate([hi, lo, hi], axis=0))
        out[0, z] = got[:YC, :XC]
        out[0, z + 1] = got[:YC, XC:]

    low[0] = out[0, :HALO]
    high[0] = out[0, ZC - HALO :]


def adjoint_y(value, before, after, wy):
    views = value.shape[0]
    view = pl.BlockSpec((1, ZC, YC, XC), lambda v: (v, 0, 0, 0))
    edge = pl.BlockSpec((1, ZC, HALO, XC), lambda v: (v, 0, 0, 0))
    face = pl.BlockSpec((1, HALO, YC, XC), lambda v: (v, 0, 0, 0))
    face_shape = jax.ShapeDtypeStruct((views, HALO, YC, XC), F32)
    return pl.pallas_call(
        adjoint_y_kernel,
        name="adjoint_y",
        grid=(views,),
        out_shape=(jax.ShapeDtypeStruct((views, ZC, YC, XC), F32), face_shape, face_shape),
        in_specs=[view, edge, edge, pl.BlockSpec((1, 32, 3 * YW), lambda v: (v, 0, 0))],
        out_specs=(view, face, face),
        compiler_params=pltpu.CompilerParams(vmem_limit_bytes=LIMIT),
    )(value, before, after, wy)


def adjoint_z_kernel(taps, value, before, after, estimate, out, win, total):
    v = pl.program_id(0)
    win[:HALO] = before[0]
    win[HALO : HALO + ZC] = value[0]
    win[HALO + ZC :] = after[0]

    @pl.when(v == 0)
    def _():
        total[...] = jnp.zeros_like(total)

    def store(z0, y0, back):
        total[pl.ds(z0, 16), y0 : y0 + 8, :] += jnp.log(back)

    z_sum(win, taps, v, store)

    @pl.when(v == VIEWS - 1)
    def _():
        out[...] = estimate[...] * jnp.exp(total[...] / VIEWS)


def adjoint_z(tz, value, before, after, estimate):
    view = pl.BlockSpec((1, ZC, YC, XC), lambda v: (v, 0, 0, 0))
    face = pl.BlockSpec((1, HALO, YC, XC), lambda v: (v, 0, 0, 0))
    chunk = pl.BlockSpec((ZC, YC, XC), lambda v: (0, 0, 0))
    return pl.pallas_call(
        adjoint_z_kernel,
        name="adjoint_z",
        grid=(VIEWS,),
        out_shape=jax.ShapeDtypeStruct((ZC, YC, XC), F32),
        in_specs=[pl.BlockSpec(memory_space=pltpu.SMEM), view, face, face, chunk],
        out_specs=chunk,
        scratch_shapes=[pltpu.VMEM((ZW, YC, XC), F32), pltpu.VMEM((ZC, YC, XC), F32)],
        compiler_params=pltpu.CompilerParams(vmem_limit_bytes=LIMIT),
    )(tz, value, before, after, estimate)


def side_columns(right, left):
    lane = lax.broadcasted_iota(jnp.int32, right.shape, right.ndim - 1)
    return jnp.where(lane < XC // 2, right, left)


def add_z(middle):
    before, after = exchange(middle[:HALO], middle[-HALO:], "z", 4)
    return jnp.concatenate([before, middle, after], axis=0)


def first_window(slab):
    padded = jnp.pad(slab, ((0, 0), (HALO, YW - HALO - YC), (XC, XC)))
    c = lax.axis_index(V)
    own, right, left = (lax.dynamic_slice_in_dim(padded, XC * (c + k), XC, axis=2) for k in (1, 2, 0))
    wide = jnp.concatenate([own, side_columns(right, left)], axis=2)
    blocks = jnp.stack([wide[:, YC * k : YC * k + YW] for k in range(SLABS)])
    planes = lax.all_to_all(blocks, S, 0, 0, tiled=True).reshape(ZC, YW, 2 * XC)
    return add_z(planes)


def next_window(chunk):
    left, right = exchange(chunk, chunk, V, VIEWS)
    wide = add_z(jnp.concatenate([chunk, side_columns(right, left)], axis=2))
    before, after = exchange(wide[:, :HALO], wide[:, YC - HALO :], S, SLABS)
    empty = jnp.zeros((ZW, YW - YC - 2 * HALO, 2 * XC), F32)
    return jnp.concatenate([before, wide, after, empty], axis=1)


def matrices(taps):
    def rows(n):
        return jnp.arange(n)[:, None]

    def columns(n):
        return jnp.arange(n)[None, :]

    k = rows(2 * XC)
    x_of = jnp.where(k < XC + XC // 2, k, k - 2 * XC)
    fx_hi, fx_lo = split_constant(banded(taps[:, 0], x_of - columns(XC) + RADIUS))
    fxa = jnp.concatenate([fx_hi, fx_lo], axis=2)
    r = columns(YW) - HALO
    fy_hi, fy_lo = split_constant(banded(taps[:, 1], r - rows(YC) + RADIUS))
    fy = jnp.concatenate([fy_hi, fy_hi, fy_lo], axis=2).reshape(VIEWS * YC, 3 * YW)
    ax_hi, ax_lo = split_constant(banded(taps[:, 0], columns(XC) - rows(XC) + RADIUS))
    own = jnp.concatenate(
        [jnp.concatenate([ax_hi, ax_lo], axis=2), jnp.concatenate([ax_hi, jnp.zeros_like(ax_lo)], axis=2)], axis=1
    )
    lane = rows(XC)
    mine = (lane // HALO)[None] == jnp.arange(VIEWS)[:, None, None]
    sides = [
        jnp.where(mine, banded(taps[:, 0], columns(XC) - at + RADIUS), 0.0)
        for at in (lane % HALO - HALO, lane % HALO + XC)
    ]
    sh_hi, sh_lo = split_constant(jnp.concatenate(sides, axis=1))
    sha = jnp.concatenate([sh_hi, sh_lo], axis=2)
    ay = jnp.pad(banded(taps[:, 1], rows(YC) - r + RADIUS), ((0, 0), (0, 32 - YC), (0, 0)))
    ay_hi, ay_lo = split_constant(ay)
    ay = jnp.concatenate([ay_hi, ay_hi, ay_lo], axis=2)
    return dict(fxa=fxa, fxb=fx_hi, fy=fy, own=own, sha=sha, shb=sh_hi, ay=ay)


def per_device(views_data, estimate, kernels):
    everyone = lax.all_gather(kernels[0], V, axis=0)
    taps = everyone / jnp.sum(everyone, axis=-1, keepdims=True)
    m = matrices(taps)
    tz, tz_flipped = taps[:, 2], taps[:, 2, ::-1]

    window = first_window(estimate)
    depth = views_data.shape[1]
    blocks = views_data[0].reshape(depth, SLABS, YC, VIEWS, XC).transpose(3, 1, 0, 2, 4)
    blocks = blocks.reshape(VIEWS * SLABS, depth, YC, XC)
    data = lax.all_to_all(blocks, V + S, 0, 0, tiled=True).reshape(VIEWS, ZC, YC, XC)
    chunk = window[HALO : HALO + ZC, HALO : HALO + YC, :XC]
    for number in range(ITERS):
        if number:
            window = next_window(chunk)
        ratio, left, right = forward(tz, window, data, m["fy"], m["fxa"], m["fxb"])
        before, after = exchange(left, right, V, VIEWS)
        value, top, bottom = adjoint_x(ratio, before, after, m["own"], m["sha"], m["shb"])
        before, after = exchange(top, bottom, S, SLABS)
        value, low, high = adjoint_y(value, before, after, m["ay"])
        before, after = exchange(low, high, "z", 4)
        chunk = adjoint_z(tz_flipped, value, before, after, chunk)

    parts = chunk.reshape(1, SLABS, depth, YC, XC)
    parts = jnp.broadcast_to(parts, (VIEWS, SLABS, depth, YC, XC)).reshape(VIEWS * SLABS, depth, YC, XC)
    got = lax.all_to_all(parts, V + S, 0, 0, tiled=True).reshape(VIEWS, SLABS, depth, YC, XC)
    return got.transpose(2, 1, 3, 0, 4).reshape(depth, SLABS * YC, VIEWS * XC)


def solution(mesh):
    fine = Mesh(mesh.devices.reshape(2, 4, 4, 2, 2), V + ("z",) + S)
    gz = ("z",) + S
    return jax.shard_map(
        per_device,
        mesh=fine,
        in_specs=(P(V, gz, None, None), P(gz, None, None), P(V, None, None)),
        out_specs=P(gz, None, None),
        check_vma=False,
    )
```

```python
import jax
import jax.numpy as jnp
from jax import lax
from jax.experimental import pallas as pl
from jax.experimental.pallas import tpu as pltpu
from jax.sharding import Mesh
from jax.sharding import PartitionSpec as P

TAPS = 31
ITERS = 2
RADIUS = 15
HALO = 16
VIEWS = 8
GROUP = 4
ZC = 64
YC = 24
XC = 128
YW = YC + 2 * HALO
YK = 64
ZW = ZC + 2 * HALO
SLABS = 4
DEPTH = ZC // SLABS
PACKED = DEPTH // 4
V = ("yh", "x")
S = ("yl", "co")
F32 = jnp.float32
BF16 = jnp.bfloat16
LIMIT = 56 * 1024 * 1024


def params(us):
    cost = pl.CostEstimate(flops=int(us * 1e9), bytes_accessed=int(us * 2e6), transcendentals=0)
    return dict(compiler_params=pltpu.CompilerParams(vmem_limit_bytes=LIMIT), cost_estimate=cost)


def split(value):
    hi = value.astype(BF16)
    return hi, (value - hi.astype(F32)).astype(BF16)


def split_constant(value):
    hi = lax.reduce_precision(value, 8, 7)
    return hi.astype(BF16), (value - hi).astype(BF16)


def dot(a, b):
    return jnp.dot(a, b, preferred_element_type=F32)


def banded(taps, offsets):
    result = jnp.zeros((taps.shape[0],) + offsets.shape, F32)
    for t in range(TAPS):
        result = result + jnp.where(offsets == t, taps[:, t, None, None], 0.0)
    return result


def exchange(low, high, axis, size):
    up = [(i, i + 1) for i in range(size - 1)]
    down = [(j, i) for i, j in up]
    return lax.ppermute(high, axis, up), lax.ppermute(low, axis, down)


def z_sum(win, taps, v, store):
    @pl.loop(0, ZC // 16)
    def _(b):
        z0 = pl.multiple_of(b * 16, 16)
        for y0 in range(0, YC, 8):
            acc = jnp.zeros((16, 8, XC), F32)
            for t in range(TAPS):
                acc = acc + taps[v, t] * win[pl.ds(z0 + t + 1, 16), y0 : y0 + 8, :]
            store(z0, y0, acc)


def forward_kernel(taps, est, data, wy, wown, wpack, ratio, left, right, yown, ypack, win):
    v = pl.program_id(0)

    @pl.when(v == 0)
    def _():
        empty = jnp.zeros((YK - YW, 2 * XC), F32)

        @pl.loop(0, SLABS + 2)
        def _(b):
            for i in range((DEPTH + PACKED) // 2):
                planes = jnp.concatenate([est[b, 2 * i], est[b, 2 * i + 1]], axis=1)
                hi, lo = split(jnp.concatenate([planes, empty], axis=0))
                got = dot(wy[...], jnp.concatenate([hi, lo, hi], axis=0))
                if i < DEPTH // 2:
                    dest, first = yown, b * DEPTH * YC + 2 * i * YC
                else:
                    dest, first = ypack, b * PACKED * YC + 2 * (i - DEPTH // 2) * YC
                rows = pl.ds(pl.multiple_of(first, 16), 2 * YC)
                for u in range(GROUP):
                    one = got[u * YC : (u + 1) * YC]
                    hi, lo = split(jnp.concatenate([one[:, :XC], one[:, XC:]], axis=0))
                    dest[u, rows, :] = jnp.concatenate([hi, lo], axis=1)

    step = 4

    @pl.loop(0, ZW // 4 // step)
    def _(b):
        rows = pl.ds(pl.multiple_of(b * step * 4 * YC, 16), step * 4 * YC)
        two = dot(yown[v, rows, :], wown[0])
        own = (two[:, :XC] + two[:, XC:]).reshape(step, 4, YC, XC)
        packed = ypack[v, pl.ds(pl.multiple_of(b * step * YC, 16), step * YC), :]
        for j in range(4):
            two = dot(packed, wpack[0, j])
            out = own[:, j] + (two[:, :XC] + two[:, XC:]).reshape(step, YC, XC)
            for q in range(step):
                win[b * step * 4 + q * 4 + j] = out[q]

    group = lax.broadcasted_iota(jnp.int32, (16, 8, XC), 2) // HALO

    def store(z0, y0, blurred):
        zs = pl.ds(z0, 16)
        value = data[0, zs, y0 : y0 + 8, :] / blurred
        ratio[0, zs, y0 : y0 + 8, :] = value
        half = z0 // (ZC // 2)
        at = GROUP * half + v
        zs = pl.ds(z0 - half * (ZC // 2), 16)
        first = pltpu.roll(value, HALO * at, 2)
        last = pltpu.roll(value, lax.rem(HALO * at + HALO, XC), 2)
        left[zs, y0 : y0 + 8, :] = jnp.where(group == at, first, left[zs, y0 : y0 + 8, :])
        right[zs, y0 : y0 + 8, :] = jnp.where(group == at, last, right[zs, y0 : y0 + 8, :])

    z_sum(win, taps, v, store)


def forward(g, tz, window, data, wy, wown, wpack):
    view = pl.BlockSpec((1, ZC, YC, XC), lambda v: (v + g * GROUP, 0, 0, 0))
    out = pl.BlockSpec((1, ZC, YC, XC), lambda v: (v, 0, 0, 0))
    pack = pl.BlockSpec((ZC // 2, YC, XC), lambda v: (0, 0, 0))
    shape = jax.ShapeDtypeStruct((ZC // 2, YC, XC), F32)
    return pl.pallas_call(
        forward_kernel,
        name="forward",
        grid=(GROUP,),
        out_shape=(jax.ShapeDtypeStruct((GROUP, ZC, YC, XC), F32), shape, shape),
        in_specs=[
            pl.BlockSpec(memory_space=pltpu.SMEM),
            pl.BlockSpec(window.shape, lambda v: (0, 0, 0, 0), pipeline_mode=pl.Buffered(1)),
            view,
            pl.BlockSpec((GROUP * YC, 3 * YK), lambda v: (g, 0), pipeline_mode=pl.Buffered(1)),
            pl.BlockSpec((1, 2 * XC, 2 * XC), lambda v: (v + g * GROUP, 0, 0)),
            pl.BlockSpec((1, 4, 2 * XC, 2 * XC), lambda v: (v + g * GROUP, 0, 0, 0)),
        ],
        out_specs=(out, pack, pack),
        scratch_shapes=[
            pltpu.VMEM((GROUP, ZW * YC, 2 * XC), BF16),
            pltpu.VMEM((GROUP, ZW // 4 * YC, 2 * XC), BF16),
            pltpu.VMEM((ZW, YC, XC), F32),
        ],
        **params(24),
    )(tz[g * GROUP : (g + 1) * GROUP], window, data, wy, wown, wpack)


def adjoint_x_kernel(ratio, before, after, wown, wha, whb, out, top, bottom):
    planes = 16

    @pl.loop(0, ZC // planes)
    def _(b):
        rows = planes * YC
        half = b // 2
        zs = pl.ds(pl.multiple_of(b * planes, planes), planes)
        hs = pl.ds(pl.multiple_of((b - 2 * half) * planes, planes), planes)
        hi, lo = split(ratio[0, zs].reshape(rows, XC))
        sides = jnp.concatenate([before[hs].reshape(rows, XC), after[hs].reshape(rows, XC)], axis=1)
        shi, slo = split(sides)
        two = dot(jnp.concatenate([hi, lo], axis=1), wown[0]) + dot(shi, wha[0, half])
        value = two[:, :XC] + two[:, XC:] + dot(slo, whb[0, half])
        value = value.reshape(planes, YC, XC)
        out[0, zs] = value
        top[0, zs] = value[:, :HALO]
        bottom[0, zs] = value[:, YC - HALO :]


def adjoint_x(g, ratio, before, after, wown, wha, whb):
    view = pl.BlockSpec((1, ZC, YC, XC), lambda v: (v, 0, 0, 0))
    pack = pl.BlockSpec((ZC // 2, YC, XC), lambda v: (0, 0, 0))
    edge = pl.BlockSpec((1, ZC, HALO, XC), lambda v: (v, 0, 0, 0))
    edge_shape = jax.ShapeDtypeStruct((GROUP, ZC, HALO, XC), F32)
    return pl.pallas_call(
        adjoint_x_kernel,
        name="adjoint_x",
        grid=(GROUP,),
        out_shape=(jax.ShapeDtypeStruct((GROUP, ZC, YC, XC), F32), edge_shape, edge_shape),
        in_specs=[
            view,
            pack,
            pack,
            pl.BlockSpec((1, 2 * XC, 2 * XC), lambda v: (v + g * GROUP, 0, 0)),
            pl.BlockSpec((1, 2, 2 * XC, 2 * XC), lambda v: (v + g * GROUP, 0, 0, 0)),
            pl.BlockSpec((1, 2, 2 * XC, XC), lambda v: (v + g * GROUP, 0, 0, 0)),
        ],
        out_specs=(view, edge, edge),
        **params(8),
    )(ratio, before, after, wown, wha, whb)


def adjoint_y_kernel(value, before, after, wy, out, low, high):
    empty = jnp.zeros((YK - YW, 2 * XC), F32)

    def pair(ref, z):
        return jnp.concatenate([ref[0, z], ref[0, z + 1]], axis=1)

    @pl.loop(0, ZC // 2, unroll=4)
    def _(b):
        z = 2 * b
        rows = jnp.concatenate([pair(before, z), pair(value, z), pair(after, z), empty], axis=0)
        hi, lo = split(rows)
        got = dot(wy[0], jnp.concatenate([hi, lo, hi], axis=0))
        out[0, z] = got[:YC, :XC]
        out[0, z + 1] = got[:YC, XC:]

    low[0] = out[0, :HALO]
    high[0] = out[0, ZC - HALO :]


def adjoint_y(g, value, before, after, wy):
    view = pl.BlockSpec((1, ZC, YC, XC), lambda v: (v, 0, 0, 0))
    edge = pl.BlockSpec((1, ZC, HALO, XC), lambda v: (v, 0, 0, 0))
    face = pl.BlockSpec((1, HALO, YC, XC), lambda v: (v, 0, 0, 0))
    face_shape = jax.ShapeDtypeStruct((GROUP, HALO, YC, XC), F32)
    return pl.pallas_call(
        adjoint_y_kernel,
        name="adjoint_y",
        grid=(GROUP,),
        out_shape=(jax.ShapeDtypeStruct((GROUP, ZC, YC, XC), F32), face_shape, face_shape),
        in_specs=[view, edge, edge, pl.BlockSpec((1, 32, 3 * YK), lambda v: (v + g * GROUP, 0, 0))],
        out_specs=(view, face, face),
        **params(8),
    )(value, before, after, wy)


def pack_sides(first, last, q):
    group = lax.broadcasted_iota(jnp.int32, first.shape[1:], 1) // HALO
    acc = jnp.zeros(first.shape[1:], F32)
    for j in range(4):
        acc = jnp.where(group == j, pltpu.roll(first[4 * q + j], HALO * j + HALO, 1), acc)
        acc = jnp.where(group == 4 + j, pltpu.roll(last[4 * q + j], XC // 2 + HALO * j, 1), acc)
    return acc


def sides_kernel(first, last, out):
    for q in range(out.shape[0]):
        out[q] = pack_sides(first, last, q)


def pack(first, last):
    return pl.pallas_call(
        sides_kernel,
        name="sides",
        out_shape=jax.ShapeDtypeStruct((first.shape[0] // 4,) + first.shape[1:], F32),
        **params(2),
    )(first, last)


def add_logs(taps, value, before, after, win, total):
    win[:HALO] = before[0]
    win[HALO : HALO + ZC] = value[0]
    win[HALO + ZC :] = after[0]

    def store(z0, y0, back):
        total[pl.ds(z0, 16), y0 : y0 + 8, :] += jnp.log(back)

    z_sum(win, taps, pl.program_id(0), store)


def first_logs_kernel(taps, value, before, after, total, win):
    @pl.when(pl.program_id(0) == 0)
    def _():
        total[...] = jnp.zeros_like(total)

    add_logs(taps, value, before, after, win, total)


def last_logs_kernel(taps, value, before, after, logs, estimate, out, sides, win, total):
    @pl.when(pl.program_id(0) == 0)
    def _():
        total[...] = logs[...]

    add_logs(taps, value, before, after, win, total)

    @pl.when(pl.program_id(0) == GROUP - 1)
    def _():
        out[...] = estimate[...] * jnp.exp(total[...] / VIEWS)

        @pl.loop(0, ZC // 4)
        def _(q):
            sides[q] = pack_sides(out, out, q)


def adjoint_z(g, tz, value, before, after, logs, estimate):
    view = pl.BlockSpec((1, ZC, YC, XC), lambda v: (v, 0, 0, 0))
    face = pl.BlockSpec((1, HALO, YC, XC), lambda v: (v, 0, 0, 0))
    chunk = pl.BlockSpec((ZC, YC, XC), lambda v: (0, 0, 0))
    packed = pl.BlockSpec((ZC // 4, YC, XC), lambda v: (0, 0, 0))
    chunk_shape = jax.ShapeDtypeStruct((ZC, YC, XC), F32)
    ins = [pl.BlockSpec(memory_space=pltpu.SMEM), view, face, face]
    win = pltpu.VMEM((ZW, YC, XC), F32)
    args = (tz[g * GROUP : (g + 1) * GROUP], value, before, after)
    if logs is None:
        return pl.pallas_call(
            first_logs_kernel,
            name="first_logs",
            grid=(GROUP,),
            out_shape=chunk_shape,
            in_specs=ins,
            out_specs=chunk,
            scratch_shapes=[win],
            **params(9),
        )(*args)
    return pl.pallas_call(
        last_logs_kernel,
        name="last_logs",
        grid=(GROUP,),
        out_shape=(chunk_shape, jax.ShapeDtypeStruct((ZC // 4, YC, XC), F32)),
        in_specs=ins + [chunk, chunk],
        out_specs=(chunk, packed),
        scratch_shapes=[win, pltpu.VMEM((ZC, YC, XC), F32)],
        **params(10),
    )(*args, logs, estimate)


def add_z(blocks):
    before, after = exchange(blocks[0], blocks[SLABS - 1], "z", 4)
    return jnp.concatenate([before[None], blocks, after[None]], axis=0)


def first_window(slab):
    padded = jnp.pad(slab, ((0, 0), (HALO, HALO), (XC, XC)))
    c = lax.axis_index(V)
    before, own, after = (lax.dynamic_slice_in_dim(padded, XC * (c + k), XC, axis=2) for k in range(3))
    planes = jnp.concatenate([own, pack(before, after)], axis=0)
    me = lax.axis_index(S)

    def rows(k):
        return lax.dynamic_slice_in_dim(planes, YC * k, YW, axis=1)

    got = [rows(me)]
    for k in range(1, SLABS):
        got.append(lax.ppermute(rows(me ^ k), S, [(i, i ^ k) for i in range(SLABS)]))
    got = jnp.stack(got)
    blocks = jnp.stack([lax.dynamic_index_in_dim(got, me ^ k, 0, keepdims=False) for k in range(SLABS)])
    return add_z(blocks), own


def next_window(chunk, sides):
    before, after = exchange(sides, sides, V, VIEWS)
    lane = lax.broadcasted_iota(jnp.int32, sides.shape, 2)
    packed = jnp.where(lane < XC // 2, before, after)
    blocks = [chunk.reshape(SLABS, DEPTH, YC, XC), packed.reshape(SLABS, PACKED, YC, XC)]
    blocks = add_z(jnp.concatenate(blocks, axis=1))
    before, after = exchange(blocks[:, :, :HALO], blocks[:, :, YC - HALO :], S, SLABS)
    return jnp.concatenate([before, blocks, after], axis=2)


def matrices(taps):
    def rows(n):
        return jnp.arange(n)[:, None]

    def columns(n):
        return jnp.arange(n)[None, :]

    def stacked(value):
        hi, lo = split_constant(value)
        top = jnp.concatenate([hi, lo], axis=-1)
        return jnp.concatenate([top, jnp.concatenate([hi, jnp.zeros_like(lo)], axis=-1)], axis=-2)

    lane = rows(XC)
    fx = stacked(banded(taps[:, 0], lane - columns(XC) + RADIUS))
    x_of = jnp.where(lane < XC // 2, lane % HALO - HALO, lane % HALO + XC)
    mine = (lane // HALO % 4)[None] == jnp.arange(4)[:, None, None]
    fp = stacked(jnp.where(mine[None], banded(taps[:, 0], x_of - columns(XC) + RADIUS)[:, None], 0.0))
    r = columns(YK) - HALO
    fy_hi, fy_lo = split_constant(banded(taps[:, 1], r - rows(YC) + RADIUS))
    fy = jnp.concatenate([fy_hi, fy_hi, fy_lo], axis=2).reshape(VIEWS * YC, 3 * YK)
    ax = stacked(banded(taps[:, 0], columns(XC) - lane + RADIUS))
    slot = GROUP * jnp.arange(2)[None, :] + (jnp.arange(VIEWS) % GROUP)[:, None]
    mine = (lane // HALO)[None, None] == slot[:, :, None, None]
    sides = [
        jnp.where(mine, banded(taps[:, 0], columns(XC) - at + RADIUS)[:, None], 0.0)
        for at in (lane % HALO - HALO, lane % HALO + XC)
    ]
    sh_hi, sh_lo = split_constant(jnp.concatenate(sides, axis=2))
    sha = jnp.concatenate([sh_hi, sh_lo], axis=3)
    ay = jnp.pad(banded(taps[:, 1], rows(YC) - r + RADIUS), ((0, 0), (0, 32 - YC), (0, 0)))
    ay_hi, ay_lo = split_constant(ay)
    ay = jnp.concatenate([ay_hi, ay_hi, ay_lo], axis=2)
    return (fy, fx, fp), (ax, sha, sh_hi), ay


def per_device(views_data, estimate, kernels):
    everyone = lax.all_gather(kernels[0], V, axis=0)
    taps = everyone / jnp.sum(everyone, axis=-1, keepdims=True)
    w_forward, w_x, w_y = matrices(taps)
    tz, tz_flipped = taps[:, 2], taps[:, 2, ::-1]

    blocks = views_data[0].reshape(DEPTH, SLABS, YC, VIEWS, XC).transpose(3, 1, 0, 2, 4)
    blocks = blocks.reshape(VIEWS * SLABS, DEPTH, YC, XC)
    data = lax.all_to_all(blocks, V + S, 0, 0, tiled=True).reshape(VIEWS, ZC, YC, XC)
    window, own = first_window(estimate)
    chunk = window[1 : 1 + SLABS, :DEPTH, HALO : HALO + YC].reshape(ZC, YC, XC)
    groups = range(VIEWS // GROUP)
    for number in range(ITERS):
        if number:
            window = next_window(chunk, sides)
        faces = []
        for g in groups:
            ratio, left, right = forward(g, tz, window, data, *w_forward)
            faces.append((ratio,) + exchange(left, right, V, VIEWS))
        edges = []
        for g in groups:
            value, top, bottom = adjoint_x(g, *faces[g], *w_x)
            edges.append((value,) + exchange(top, bottom, S, SLABS))
        ends = []
        for g in groups:
            value, low, high = adjoint_y(g, *edges[g], w_y)
            ends.append((value,) + exchange(low, high, "z", 4))
        logs = adjoint_z(0, tz_flipped, *ends[0], None, None)
        chunk, sides = adjoint_z(1, tz_flipped, *ends[1], logs, chunk)

    parts = chunk.reshape(1, SLABS, DEPTH, YC, XC)
    parts = jnp.broadcast_to(parts, (VIEWS, SLABS, DEPTH, YC, XC)).reshape(VIEWS * SLABS, DEPTH, YC, XC)
    got = lax.all_to_all(parts, V + S, 0, 0, tiled=True).reshape(VIEWS, SLABS, DEPTH, YC, XC)
    return got.transpose(2, 1, 3, 0, 4).reshape(DEPTH, SLABS * YC, VIEWS * XC)


def solution(mesh):
    fine = Mesh(mesh.devices.reshape(2, 4, 4, 2, 2), V + ("z",) + S)
    gz = ("z",) + S
    return jax.shard_map(
        per_device,
        mesh=fine,
        in_specs=(P(V, gz, None, None), P(gz, None, None), P(V, None, None)),
        out_specs=P(gz, None, None),
        check_vma=False,
    )
```

```python
import functools

import jax
import jax.numpy as jnp
from jax import lax
from jax.experimental import pallas as pl
from jax.experimental.pallas import tpu as pltpu
from jax.sharding import Mesh
from jax.sharding import PartitionSpec as P

TAPS = 31
ITERS = 2
RADIUS = 15
HALO = 16
VIEWS = 8
GROUP = 4
ZC = 64
YC = 24
XC = 128
YW = YC + 2 * HALO
YK = 64
ZW = ZC + 2 * HALO
SLABS = 4
DEPTH = ZC // SLABS
PACKED = DEPTH // 4
V = ("yh", "x")
S = ("yl", "co")
F32 = jnp.float32
BF16 = jnp.bfloat16
LIMIT = 56 * 1024 * 1024


def params(us):
    cost = pl.CostEstimate(flops=int(us * 1e9), bytes_accessed=int(us * 2e6), transcendentals=0)
    return dict(compiler_params=pltpu.CompilerParams(vmem_limit_bytes=LIMIT), cost_estimate=cost)


def split(value):
    hi = value.astype(BF16)
    return hi, (value - hi.astype(F32)).astype(BF16)


def dot(a, b):
    return jnp.dot(a, b, preferred_element_type=F32)


def banded(taps, v, axis, offsets):
    result = jnp.zeros(offsets.shape, F32)
    for t in range(TAPS):
        result = jnp.where(offsets == t, taps[v, axis * TAPS + t], result)
    return result


def exchange(low, high, axis, size):
    up = [(i, i + 1) for i in range(size - 1)]
    down = [(j, i) for i, j in up]
    return lax.ppermute(high, axis, up), lax.ppermute(low, axis, down)


def z_sum(win, taps, v, flipped, store):
    @pl.loop(0, ZC // 16)
    def _(b):
        z0 = pl.multiple_of(b * 16, 16)
        for y0 in range(0, YC, 8):
            acc = jnp.zeros((16, 8, XC), F32)
            for t in range(TAPS):
                tap = taps[v, 2 * TAPS + (TAPS - 1 - t if flipped else t)]
                acc = acc + tap * win[pl.ds(z0 + t + 1, 16), y0 : y0 + 8, :]
            store(z0, y0, acc)


def blur_planes(g, taps, est, wy, wown, wpack, yown, ypack, win):
    v = pl.program_id(0)

    @pl.when(v == 0)
    def _():
        empty = jnp.zeros((YK - YW, 2 * XC), F32)
        matrix = wy[...].astype(BF16)

        @pl.loop(0, SLABS + 2)
        def _(b):
            for i in range((DEPTH + PACKED) // 2):
                planes = jnp.concatenate([est[b, 2 * i], est[b, 2 * i + 1]], axis=1)
                hi, lo = split(jnp.concatenate([planes, empty], axis=0))
                got = dot(matrix, jnp.concatenate([hi, lo, hi], axis=0))
                if i < DEPTH // 2:
                    dest, first = yown, b * DEPTH * YC + 2 * i * YC
                else:
                    dest, first = ypack, b * PACKED * YC + 2 * (i - DEPTH // 2) * YC
                rows = pl.ds(pl.multiple_of(first, 16), 2 * YC)
                for u in range(GROUP):
                    one = got[u * YC : (u + 1) * YC]
                    hi, lo = split(jnp.concatenate([one[:, :XC], one[:, XC:]], axis=0))
                    dest[u, rows, :] = jnp.concatenate([hi, lo], axis=1)

    step = 4

    @pl.loop(0, ZW // 4 // step)
    def _(b):
        rows = pl.ds(pl.multiple_of(b * step * 4 * YC, 16), step * 4 * YC)
        two = dot(yown[v, rows, :], wown[0])
        own = (two[:, :XC] + two[:, XC:]).reshape(step, 4, YC, XC)
        packed = ypack[v, pl.ds(pl.multiple_of(b * step * YC, 16), step * YC), :]
        for j in range(4):
            two = dot(packed, wpack[0, j])
            out = own[:, j] + (two[:, :XC] + two[:, XC:]).reshape(step, YC, XC)
            for q in range(step):
                win[b * step * 4 + q * 4 + j] = out[q]


def divide(z0, y0, recorded, blurred, ratio, left, right):
    v = pl.program_id(0)
    zs, ys = pl.ds(z0, 16), pl.ds(y0, 8)
    value = recorded[0, zs, ys, :] / blurred
    ratio[0, zs, ys, :] = value
    half = z0 // (ZC // 2)
    at = GROUP * half + v
    mine = lax.broadcasted_iota(jnp.int32, value.shape, 2) // HALO == at
    zs = pl.ds(z0 - half * (ZC // 2), 16)
    first = pltpu.roll(value, HALO * at, 2)
    last = pltpu.roll(value, lax.rem(HALO * at + HALO, XC), 2)
    left[zs, ys, :] = jnp.where(mine, first, left[zs, ys, :])
    right[zs, ys, :] = jnp.where(mine, last, right[zs, ys, :])


def blur_kernel(g, taps, est, wy, wown, wpack, blurred, yown, ypack, win):
    blur_planes(g, taps, est, wy, wown, wpack, yown, ypack, win)

    def store(z0, y0, value):
        blurred[0, pl.ds(z0, 16), y0 : y0 + 8, :] = value

    z_sum(win, taps, g * GROUP + pl.program_id(0), False, store)


def blur_and_divide_kernel(g, taps, est, wy, wown, wpack, data, ratio, left, right, yown, ypack, win):
    blur_planes(g, taps, est, wy, wown, wpack, yown, ypack, win)

    def store(z0, y0, value):
        divide(z0, y0, data, value, ratio, left, right)

    z_sum(win, taps, g * GROUP + pl.program_id(0), False, store)


def divide_kernel(data, blurred, ratio, left, right):
    @pl.loop(0, ZC // 16)
    def _(b):
        z0 = pl.multiple_of(b * 16, 16)
        for y0 in range(0, YC, 8):
            divide(z0, y0, data, blurred[0, pl.ds(z0, 16), y0 : y0 + 8, :], ratio, left, right)


def of_view(g, *shape):
    return pl.BlockSpec((1,) + shape, lambda v: (v + g * GROUP,) + (0,) * len(shape))


OUT_VIEW = pl.BlockSpec((1, ZC, YC, XC), lambda v: (v, 0, 0, 0))
OUT_SIDES = pl.BlockSpec((ZC // 2, YC, XC), lambda v: (0, 0, 0))
VIEW_SHAPE = jax.ShapeDtypeStruct((GROUP, ZC, YC, XC), F32)
SIDES_SHAPE = jax.ShapeDtypeStruct((ZC // 2, YC, XC), F32)


def forward(g, taps, window, data, wy, wown, wpack):
    ins = [
        pl.BlockSpec(memory_space=pltpu.SMEM),
        pl.BlockSpec(window.shape, lambda v: (0, 0, 0, 0), pipeline_mode=pl.Buffered(1)),
        pl.BlockSpec((GROUP * YC, 3 * YK), lambda v: (g, 0), pipeline_mode=pl.Buffered(1)),
        of_view(g, 2 * XC, 2 * XC),
        of_view(g, 4, 2 * XC, 2 * XC),
    ]
    scratch = [
        pltpu.VMEM((GROUP, ZW * YC, 2 * XC), BF16),
        pltpu.VMEM((GROUP, ZW // 4 * YC, 2 * XC), BF16),
        pltpu.VMEM((ZW, YC, XC), F32),
    ]
    if data is None:
        return pl.pallas_call(
            functools.partial(blur_kernel, g),
            name="blur",
            grid=(GROUP,),
            out_shape=VIEW_SHAPE,
            in_specs=ins,
            out_specs=OUT_VIEW,
            scratch_shapes=scratch,
            **params(18),
        )(taps, window, wy, wown, wpack)
    return pl.pallas_call(
        functools.partial(blur_and_divide_kernel, g),
        name="blur_and_divide",
        grid=(GROUP,),
        out_shape=(VIEW_SHAPE, SIDES_SHAPE, SIDES_SHAPE),
        in_specs=ins + [of_view(g, ZC, YC, XC)],
        out_specs=(OUT_VIEW, OUT_SIDES, OUT_SIDES),
        scratch_shapes=scratch,
        **params(24),
    )(taps, window, wy, wown, wpack, data)


def divide_by(g, data, blurred):
    return pl.pallas_call(
        divide_kernel,
        name="divide",
        grid=(GROUP,),
        out_shape=(VIEW_SHAPE, SIDES_SHAPE, SIDES_SHAPE),
        in_specs=[of_view(g, ZC, YC, XC), OUT_VIEW],
        out_specs=(OUT_VIEW, OUT_SIDES, OUT_SIDES),
        **params(5),
    )(data, blurred)


def adjoint_x_kernel(ratio, before, after, wown, wha, whb, out, top, bottom):
    planes = 16

    @pl.loop(0, ZC // planes)
    def _(b):
        rows = planes * YC
        half = b // 2
        zs = pl.ds(pl.multiple_of(b * planes, planes), planes)
        hs = pl.ds(pl.multiple_of((b - 2 * half) * planes, planes), planes)
        hi, lo = split(ratio[0, zs].reshape(rows, XC))
        sides = jnp.concatenate([before[hs].reshape(rows, XC), after[hs].reshape(rows, XC)], axis=1)
        shi, slo = split(sides)
        two = dot(jnp.concatenate([hi, lo], axis=1), wown[0]) + dot(shi, wha[0, half])
        value = two[:, :XC] + two[:, XC:] + dot(slo, whb[0, half])
        value = value.reshape(planes, YC, XC)
        out[0, zs] = value
        top[0, zs] = value[:, :HALO]
        bottom[0, zs] = value[:, YC - HALO :]


def adjoint_x(g, ratio, before, after, wown, wha, whb):
    view = pl.BlockSpec((1, ZC, YC, XC), lambda v: (v, 0, 0, 0))
    pack = pl.BlockSpec((ZC // 2, YC, XC), lambda v: (0, 0, 0))
    edge = pl.BlockSpec((1, ZC, HALO, XC), lambda v: (v, 0, 0, 0))
    edge_shape = jax.ShapeDtypeStruct((GROUP, ZC, HALO, XC), F32)
    return pl.pallas_call(
        adjoint_x_kernel,
        name="adjoint_x",
        grid=(GROUP,),
        out_shape=(jax.ShapeDtypeStruct((GROUP, ZC, YC, XC), F32), edge_shape, edge_shape),
        in_specs=[
            view,
            pack,
            pack,
            pl.BlockSpec((1, 2 * XC, 2 * XC), lambda v: (v + g * GROUP, 0, 0)),
            pl.BlockSpec((1, 2, 2 * XC, 2 * XC), lambda v: (v + g * GROUP, 0, 0, 0)),
            pl.BlockSpec((1, 2, 2 * XC, XC), lambda v: (v + g * GROUP, 0, 0, 0)),
        ],
        out_specs=(view, edge, edge),
        **params(8),
    )(ratio, before, after, wown, wha, whb)


def adjoint_y_kernel(value, before, after, wy, out, low, high):
    empty = jnp.zeros((YK - YW, 2 * XC), F32)

    def pair(ref, z):
        return jnp.concatenate([ref[0, z], ref[0, z + 1]], axis=1)

    @pl.loop(0, ZC // 2, unroll=4)
    def _(b):
        z = 2 * b
        rows = jnp.concatenate([pair(before, z), pair(value, z), pair(after, z), empty], axis=0)
        hi, lo = split(rows)
        got = dot(wy[0], jnp.concatenate([hi, lo, hi], axis=0))
        out[0, z] = got[:YC, :XC]
        out[0, z + 1] = got[:YC, XC:]

    low[0] = out[0, :HALO]
    high[0] = out[0, ZC - HALO :]


def adjoint_y(g, value, before, after, wy):
    view = pl.BlockSpec((1, ZC, YC, XC), lambda v: (v, 0, 0, 0))
    edge = pl.BlockSpec((1, ZC, HALO, XC), lambda v: (v, 0, 0, 0))
    face = pl.BlockSpec((1, HALO, YC, XC), lambda v: (v, 0, 0, 0))
    face_shape = jax.ShapeDtypeStruct((GROUP, HALO, YC, XC), F32)
    return pl.pallas_call(
        adjoint_y_kernel,
        name="adjoint_y",
        grid=(GROUP,),
        out_shape=(jax.ShapeDtypeStruct((GROUP, ZC, YC, XC), F32), face_shape, face_shape),
        in_specs=[view, edge, edge, pl.BlockSpec((1, 32, 3 * YK), lambda v: (v + g * GROUP, 0, 0))],
        out_specs=(view, face, face),
        **params(8),
    )(value, before, after, wy)


def pack_sides(first, last, q):
    group = lax.broadcasted_iota(jnp.int32, first.shape[1:], 1) // HALO
    acc = jnp.zeros(first.shape[1:], F32)
    for j in range(4):
        acc = jnp.where(group == j, pltpu.roll(first[4 * q + j], HALO * j + HALO, 1), acc)
        acc = jnp.where(group == 4 + j, pltpu.roll(last[4 * q + j], XC // 2 + HALO * j, 1), acc)
    return acc


def sides_kernel(first, last, out):
    for q in range(out.shape[0]):
        out[q] = pack_sides(first, last, q)


def pack(first, last):
    return pl.pallas_call(
        sides_kernel,
        name="sides",
        out_shape=jax.ShapeDtypeStruct((first.shape[0] // 4,) + first.shape[1:], F32),
        **params(1),
    )(first, last)


def add_logs(g, taps, value, before, after, win, total):
    win[:HALO] = before[0]
    win[HALO : HALO + ZC] = value[0]
    win[HALO + ZC :] = after[0]

    def store(z0, y0, back):
        total[pl.ds(z0, 16), y0 : y0 + 8, :] += jnp.log(back)

    z_sum(win, taps, g * GROUP + pl.program_id(0), True, store)


def first_logs_kernel(g, taps, value, before, after, total, win):
    @pl.when(pl.program_id(0) == 0)
    def _():
        total[...] = jnp.zeros_like(total)

    add_logs(g, taps, value, before, after, win, total)


def last_logs_kernel(g, taps, value, before, after, logs, estimate, out, sides, win, total):
    @pl.when(pl.program_id(0) == 0)
    def _():
        total[...] = logs[...]

    add_logs(g, taps, value, before, after, win, total)

    @pl.when(pl.program_id(0) == GROUP - 1)
    def _():
        out[...] = estimate[...] * jnp.exp(total[...] / VIEWS)

        @pl.loop(0, ZC // 4)
        def _(q):
            sides[q] = pack_sides(out, out, q)


def adjoint_z(g, taps, value, before, after, logs, estimate):
    view = pl.BlockSpec((1, ZC, YC, XC), lambda v: (v, 0, 0, 0))
    face = pl.BlockSpec((1, HALO, YC, XC), lambda v: (v, 0, 0, 0))
    chunk = pl.BlockSpec((ZC, YC, XC), lambda v: (0, 0, 0))
    packed = pl.BlockSpec((ZC // 4, YC, XC), lambda v: (0, 0, 0))
    chunk_shape = jax.ShapeDtypeStruct((ZC, YC, XC), F32)
    ins = [pl.BlockSpec(memory_space=pltpu.SMEM), view, face, face]
    win = pltpu.VMEM((ZW, YC, XC), F32)
    args = (taps, value, before, after)
    if logs is None:
        return pl.pallas_call(
            functools.partial(first_logs_kernel, g),
            name="first_logs",
            grid=(GROUP,),
            out_shape=chunk_shape,
            in_specs=ins,
            out_specs=chunk,
            scratch_shapes=[win],
            **params(9),
        )(*args)
    return pl.pallas_call(
        functools.partial(last_logs_kernel, g),
        name="last_logs",
        grid=(GROUP,),
        out_shape=(chunk_shape, jax.ShapeDtypeStruct((ZC // 4, YC, XC), F32)),
        in_specs=ins + [chunk, chunk],
        out_specs=(chunk, packed),
        scratch_shapes=[win, pltpu.VMEM((ZC, YC, XC), F32)],
        **params(10),
    )(*args, logs, estimate)


def add_z(blocks):
    before, after = exchange(blocks[0], blocks[SLABS - 1], "z", 4)
    return jnp.concatenate([before[None], blocks, after[None]], axis=0)


def first_window(slab):
    padded = jnp.pad(slab, ((0, 0), (HALO, HALO), (XC, XC)))
    c = lax.axis_index(V)
    before, own, after = (lax.dynamic_slice_in_dim(padded, XC * (c + k), XC, axis=2) for k in range(3))
    planes = jnp.concatenate([own, pack(before, after)], axis=0)
    me = lax.axis_index(S)

    def rows(k):
        return lax.dynamic_slice_in_dim(planes, YC * k, YW, axis=1)

    got = [rows(me)]
    for k in range(1, SLABS):
        got.append(lax.ppermute(rows(me ^ k), S, [(i, i ^ k) for i in range(SLABS)]))
    got = jnp.stack(got)
    blocks = jnp.stack([lax.dynamic_index_in_dim(got, me ^ k, 0, keepdims=False) for k in range(SLABS)])
    return add_z(blocks)


def next_window(chunk, sides):
    before, after = exchange(sides, sides, V, VIEWS)
    lane = lax.broadcasted_iota(jnp.int32, sides.shape, 2)
    packed = jnp.where(lane < XC // 2, before, after)
    blocks = [chunk.reshape(SLABS, DEPTH, YC, XC), packed.reshape(SLABS, PACKED, YC, XC)]
    blocks = add_z(jnp.concatenate(blocks, axis=1))
    before, after = exchange(blocks[:, :, :HALO], blocks[:, :, YC - HALO :], S, SLABS)
    return jnp.concatenate([before, blocks, after], axis=2)


def matrices_kernel(taps, fy, fx, fp, ax, sha, shb, ay):
    v = pl.program_id(0)

    def row_column(rows, columns):
        return tuple(lax.broadcasted_iota(jnp.int32, (rows, columns), d) for d in range(2))

    def stacked(ref, at, value):
        hi, lo = split(value)
        ref[at + (slice(0, XC), slice(0, XC))] = hi
        ref[at + (slice(0, XC), slice(XC, 2 * XC))] = lo
        ref[at + (slice(XC, 2 * XC), slice(0, XC))] = hi
        ref[at + (slice(XC, 2 * XC), slice(XC, 2 * XC))] = jnp.zeros_like(lo)

    def along_y(value):
        hi, lo = split(value)
        column = row_column(*value.shape)[1]
        return jnp.where(column < 2 * YK, hi.astype(F32), lo.astype(F32))

    r, c = row_column(XC, XC)
    stacked(fx, (0,), banded(taps, v, 0, r - c + RADIUS))
    stacked(ax, (0,), banded(taps, v, 0, c - r + RADIUS))
    x_of = jnp.where(r < XC // 2, r % HALO - HALO, r % HALO + XC)
    packed = banded(taps, v, 0, x_of - c + RADIUS)
    for j in range(4):
        stacked(fp, (0, j), jnp.where(r // HALO % 4 == j, packed, 0.0))
    for side, x_of in enumerate((r % HALO - HALO, r % HALO + XC)):
        values = banded(taps, v, 0, c - x_of + RADIUS)
        rows = slice(side * XC, (side + 1) * XC)
        for half in range(2):
            hi, lo = split(jnp.where(r // HALO == GROUP * half + v % GROUP, values, 0.0))
            sha[0, half, rows, :XC] = hi
            sha[0, half, rows, XC:] = lo
            shb[0, half, rows, :] = hi
    r, c = row_column(YC, 3 * YK)
    fy[...] = along_y(banded(taps, v, 1, c % YK - HALO - r + RADIUS))
    r, c = row_column(32, 3 * YK)
    values = banded(taps, v, 1, r - (c % YK - HALO) + RADIUS)
    ay[0] = along_y(jnp.where(r < YC, values, 0.0)).astype(BF16)


def matrices(taps):
    shapes = [
        (2 * XC, 2 * XC),
        (4, 2 * XC, 2 * XC),
        (2 * XC, 2 * XC),
        (2, 2 * XC, 2 * XC),
        (2, 2 * XC, XC),
        (32, 3 * YK),
    ]
    fy, fx, fp, ax, sha, shb, ay = pl.pallas_call(
        matrices_kernel,
        name="matrices",
        grid=(VIEWS,),
        out_shape=[jax.ShapeDtypeStruct((VIEWS * YC, 3 * YK), F32)]
        + [jax.ShapeDtypeStruct((VIEWS,) + shape, BF16) for shape in shapes],
        in_specs=[pl.BlockSpec(memory_space=pltpu.SMEM)],
        out_specs=[pl.BlockSpec((YC, 3 * YK), lambda v: (v, 0))] + [of_view(0, *shape) for shape in shapes],
        **params(1),
    )(taps)
    return (fy, fx, fp), (ax, sha, shb), ay


def spread_kernel(got, out):
    for c in range(VIEWS):
        for y in range(SLABS):
            out[:, y * YC : (y + 1) * YC, c * XC : (c + 1) * XC] = got[c, y]


def spread(got):
    planes = 2
    return pl.pallas_call(
        spread_kernel,
        name="spread",
        grid=(DEPTH // planes,),
        out_shape=jax.ShapeDtypeStruct((DEPTH, SLABS * YC, VIEWS * XC), F32),
        in_specs=[pl.BlockSpec((VIEWS, SLABS, planes, YC, XC), lambda b: (0, 0, b, 0, 0))],
        out_specs=pl.BlockSpec((planes, SLABS * YC, VIEWS * XC), lambda b: (b, 0, 0)),
        **params(5),
    )(got)


def per_device(views_data, estimate, kernels):
    everyone = lax.all_gather(kernels[0], V, axis=0)
    views_data, estimate, everyone = lax.optimization_barrier((views_data, estimate, everyone))
    taps = (everyone / jnp.sum(everyone, axis=-1, keepdims=True)).reshape(VIEWS, 3 * TAPS)
    w_forward, w_x, w_y = matrices(taps)

    blocks = views_data[0].reshape(DEPTH, SLABS, YC, VIEWS, XC).transpose(3, 1, 0, 2, 4)
    blocks = blocks.reshape(VIEWS * SLABS, DEPTH, YC, XC)
    data = lax.all_to_all(blocks, V + S, 0, 0, tiled=True).reshape(VIEWS, ZC, YC, XC)
    window = first_window(estimate)
    chunk = window[1 : 1 + SLABS, :DEPTH, HALO : HALO + YC].reshape(ZC, YC, XC)
    groups = range(VIEWS // GROUP)
    for number in range(ITERS):
        if number:
            window = next_window(chunk, sides)
        if not number:
            blurred = [forward(g, taps, window, None, *w_forward) for g in groups]
        faces = []
        for g in groups:
            if number:
                ratio, left, right = forward(g, taps, window, data, *w_forward)
            else:
                ratio, left, right = divide_by(g, data, blurred[g])
            faces.append((ratio,) + exchange(left, right, V, VIEWS))
        edges = []
        for g in groups:
            value, top, bottom = adjoint_x(g, *faces[g], *w_x)
            edges.append((value,) + exchange(top, bottom, S, SLABS))
        ends = []
        for g in groups:
            value, low, high = adjoint_y(g, *edges[g], w_y)
            ends.append((value,) + exchange(low, high, "z", 4))
        logs = adjoint_z(0, taps, *ends[0], None, None)
        chunk, sides = adjoint_z(1, taps, *ends[1], logs, chunk)

    parts = chunk.reshape(1, SLABS, DEPTH, YC, XC)
    parts = jnp.broadcast_to(parts, (VIEWS, SLABS, DEPTH, YC, XC)).reshape(VIEWS * SLABS, DEPTH, YC, XC)
    got = lax.all_to_all(parts, V + S, 0, 0, tiled=True).reshape(VIEWS, SLABS, DEPTH, YC, XC)
    return spread(got)


def solution(mesh):
    fine = Mesh(mesh.devices.reshape(2, 4, 4, 2, 2), V + ("z",) + S)
    gz = ("z",) + S
    return jax.shard_map(
        per_device,
        mesh=fine,
        in_specs=(P(V, gz, None, None), P(gz, None, None), P(V, None, None)),
        out_specs=P(gz, None, None),
        check_vma=False,
    )
```

```python
import functools

import jax
import jax.numpy as jnp
from jax import lax
from jax.experimental import pallas as pl
from jax.experimental.pallas import tpu as pltpu
from jax.sharding import Mesh
from jax.sharding import PartitionSpec as P

TAPS = 31
ITERS = 2
RADIUS = 15
HALO = 16
VIEWS = 8
GROUP = 4
ZC = 64
YC = 24
XC = 128
YW = YC + 2 * HALO
YK = 64
ZW = ZC + 2 * HALO
SLABS = 4
DEPTH = ZC // SLABS
PACKED = DEPTH // 4
V = ("yh", "x")
S = ("yl", "co")
F32 = jnp.float32
BF16 = jnp.bfloat16
LIMIT = 56 * 1024 * 1024


def params(us):
    cost = pl.CostEstimate(flops=int(us * 1e9), bytes_accessed=int(us * 2e6), transcendentals=0)
    return dict(compiler_params=pltpu.CompilerParams(vmem_limit_bytes=LIMIT), cost_estimate=cost)


def split(value):
    hi = value.astype(BF16)
    return hi, (value - hi.astype(F32)).astype(BF16)


def dot(a, b):
    return jnp.dot(a, b, preferred_element_type=F32)


def banded(taps, v, axis, offsets):
    result = jnp.zeros(offsets.shape, F32)
    for t in range(TAPS):
        result = jnp.where(offsets == t, taps[v, axis * TAPS + t], result)
    return result


def exchange(low, high, axis, size):
    up = [(i, i + 1) for i in range(size - 1)]
    down = [(j, i) for i, j in up]
    return lax.ppermute(high, axis, up), lax.ppermute(low, axis, down)


def z_sum(win, taps, v, flipped, store):
    @pl.loop(0, ZC // 16)
    def _(b):
        z0 = pl.multiple_of(b * 16, 16)
        for y0 in range(0, YC, 8):
            acc = jnp.zeros((16, 8, XC), F32)
            for t in range(TAPS):
                tap = taps[v, 2 * TAPS + (TAPS - 1 - t if flipped else t)]
                acc = acc + tap * win[pl.ds(z0 + t + 1, 16), y0 : y0 + 8, :]
            store(z0, y0, acc)


def blur_planes(g, taps, est, wy, wown, wpack, yown, ypack, win):
    v = pl.program_id(0)

    @pl.when(v == 0)
    def _():
        empty = jnp.zeros((YK - YW, 2 * XC), F32)
        matrix = wy[...].astype(BF16)

        @pl.loop(0, SLABS + 2)
        def _(b):
            for i in range((DEPTH + PACKED) // 2):
                planes = jnp.concatenate([est[b, 2 * i], est[b, 2 * i + 1]], axis=1)
                hi, lo = split(jnp.concatenate([planes, empty], axis=0))
                got = dot(matrix, jnp.concatenate([hi, lo, hi], axis=0))
                if i < DEPTH // 2:
                    dest, first = yown, b * DEPTH * YC + 2 * i * YC
                else:
                    dest, first = ypack, b * PACKED * YC + 2 * (i - DEPTH // 2) * YC
                rows = pl.ds(pl.multiple_of(first, 16), 2 * YC)
                for u in range(GROUP):
                    one = got[u * YC : (u + 1) * YC]
                    hi, lo = split(jnp.concatenate([one[:, :XC], one[:, XC:]], axis=0))
                    dest[u, rows, :] = jnp.concatenate([hi, lo], axis=1)

    step = 4

    @pl.loop(0, ZW // 4 // step)
    def _(b):
        rows = pl.ds(pl.multiple_of(b * step * 4 * YC, 16), step * 4 * YC)
        two = dot(yown[v, rows, :], wown[0])
        own = (two[:, :XC] + two[:, XC:]).reshape(step, 4, YC, XC)
        packed = ypack[v, pl.ds(pl.multiple_of(b * step * YC, 16), step * YC), :]
        for j in range(4):
            two = dot(packed, wpack[0, j])
            out = own[:, j] + (two[:, :XC] + two[:, XC:]).reshape(step, YC, XC)
            for q in range(step):
                win[b * step * 4 + q * 4 + j] = out[q]


def divide(z0, y0, recorded, blurred, ratio, left, right):
    v = pl.program_id(0)
    zs, ys = pl.ds(z0, 16), pl.ds(y0, 8)
    value = recorded[0, zs, ys, :] / blurred
    ratio[0, zs, ys, :] = value
    half = z0 // (ZC // 2)
    slot = lax.broadcasted_iota(jnp.int32, value.shape, 2) // HALO
    zs = pl.ds(z0 - half * (ZC // 2), 16)
    at = GROUP * (1 - half) + v
    first = pltpu.roll(value, HALO * at, 2)
    left[zs, ys, :] = jnp.where(slot == at, first, left[zs, ys, :])
    at = GROUP * half + v
    last = pltpu.roll(value, lax.rem(HALO * at + HALO, XC), 2)
    right[zs, ys, :] = jnp.where(slot == at, last, right[zs, ys, :])


def blur_kernel(g, taps, est, wy, wown, wpack, blurred, yown, ypack, win):
    blur_planes(g, taps, est, wy, wown, wpack, yown, ypack, win)

    def store(z0, y0, value):
        blurred[0, pl.ds(z0, 16), y0 : y0 + 8, :] = value

    z_sum(win, taps, g * GROUP + pl.program_id(0), False, store)


def blur_and_divide_kernel(g, taps, est, wy, wown, wpack, data, ratio, left, right, yown, ypack, win):
    blur_planes(g, taps, est, wy, wown, wpack, yown, ypack, win)

    def store(z0, y0, value):
        divide(z0, y0, data, value, ratio, left, right)

    z_sum(win, taps, g * GROUP + pl.program_id(0), False, store)


def divide_kernel(data, blurred, ratio, left, right):
    @pl.loop(0, ZC // 16)
    def _(b):
        z0 = pl.multiple_of(b * 16, 16)
        for y0 in range(0, YC, 8):
            divide(z0, y0, data, blurred[0, pl.ds(z0, 16), y0 : y0 + 8, :], ratio, left, right)


def of_view(g, *shape):
    return pl.BlockSpec((1,) + shape, lambda v: (v + g * GROUP,) + (0,) * len(shape))


OUT_VIEW = pl.BlockSpec((1, ZC, YC, XC), lambda v: (v, 0, 0, 0))
OUT_SIDES = pl.BlockSpec((ZC // 2, YC, XC), lambda v: (0, 0, 0))
VIEW_SHAPE = jax.ShapeDtypeStruct((GROUP, ZC, YC, XC), F32)
SIDES_SHAPE = jax.ShapeDtypeStruct((ZC // 2, YC, XC), F32)


def forward(g, taps, window, data, wy, wown, wpack):
    ins = [
        pl.BlockSpec(memory_space=pltpu.SMEM),
        pl.BlockSpec(window.shape, lambda v: (0, 0, 0, 0), pipeline_mode=pl.Buffered(1)),
        pl.BlockSpec((GROUP * YC, 3 * YK), lambda v: (g, 0), pipeline_mode=pl.Buffered(1)),
        of_view(g, 2 * XC, 2 * XC),
        of_view(g, 4, 2 * XC, 2 * XC),
    ]
    scratch = [
        pltpu.VMEM((GROUP, ZW * YC, 2 * XC), BF16),
        pltpu.VMEM((GROUP, ZW // 4 * YC, 2 * XC), BF16),
        pltpu.VMEM((ZW, YC, XC), F32),
    ]
    if data is None:
        return pl.pallas_call(
            functools.partial(blur_kernel, g),
            name="blur",
            grid=(GROUP,),
            out_shape=VIEW_SHAPE,
            in_specs=ins,
            out_specs=OUT_VIEW,
            scratch_shapes=scratch,
            **params(18),
        )(taps, window, wy, wown, wpack)
    return pl.pallas_call(
        functools.partial(blur_and_divide_kernel, g),
        name="blur_and_divide",
        grid=(GROUP,),
        out_shape=(VIEW_SHAPE, SIDES_SHAPE, SIDES_SHAPE),
        in_specs=ins + [of_view(g, ZC, YC, XC)],
        out_specs=(OUT_VIEW, OUT_SIDES, OUT_SIDES),
        scratch_shapes=scratch,
        **params(24),
    )(taps, window, wy, wown, wpack, data)


def divide_by(g, data, blurred):
    return pl.pallas_call(
        divide_kernel,
        name="divide",
        grid=(GROUP,),
        out_shape=(VIEW_SHAPE, SIDES_SHAPE, SIDES_SHAPE),
        in_specs=[of_view(g, ZC, YC, XC), OUT_VIEW],
        out_specs=(OUT_VIEW, OUT_SIDES, OUT_SIDES),
        **params(5),
    )(data, blurred)


def adjoint_x_kernel(ratio, before, after, wown, wside, out, top, bottom):
    planes = 16
    low_lanes = lax.broadcasted_iota(jnp.int32, (planes * YC, XC), 1) < XC // 2

    @pl.loop(0, ZC // planes)
    def _(b):
        rows = planes * YC
        half = b // 2
        zs = pl.ds(pl.multiple_of(b * planes, planes), planes)
        hs = pl.ds(pl.multiple_of((b - 2 * half) * planes, planes), planes)
        hi, lo = split(ratio[0, zs].reshape(rows, XC))
        is_before = low_lanes == (half == 0)
        shi, slo = split(jnp.where(is_before, before[hs].reshape(rows, XC), after[hs].reshape(rows, XC)))
        two = dot(jnp.concatenate([hi, lo], axis=1), wown[0])
        two = two + dot(jnp.concatenate([shi, slo], axis=1), wside[0, half])
        value = two[:, :XC] + two[:, XC:]
        value = value.reshape(planes, YC, XC)
        out[0, zs] = value
        top[0, zs] = value[:, :HALO]
        bottom[0, zs] = value[:, YC - HALO :]


def adjoint_x(g, ratio, before, after, wown, wside):
    view = pl.BlockSpec((1, ZC, YC, XC), lambda v: (v, 0, 0, 0))
    pack = pl.BlockSpec((ZC // 2, YC, XC), lambda v: (0, 0, 0))
    edge = pl.BlockSpec((1, ZC, HALO, XC), lambda v: (v, 0, 0, 0))
    edge_shape = jax.ShapeDtypeStruct((GROUP, ZC, HALO, XC), F32)
    return pl.pallas_call(
        adjoint_x_kernel,
        name="adjoint_x",
        grid=(GROUP,),
        out_shape=(jax.ShapeDtypeStruct((GROUP, ZC, YC, XC), F32), edge_shape, edge_shape),
        in_specs=[
            view,
            pack,
            pack,
            pl.BlockSpec((1, 2 * XC, 2 * XC), lambda v: (v + g * GROUP, 0, 0)),
            pl.BlockSpec((1, 2, 2 * XC, 2 * XC), lambda v: (v + g * GROUP, 0, 0, 0)),
        ],
        out_specs=(view, edge, edge),
        **params(8),
    )(ratio, before, after, wown, wside)


def adjoint_y_kernel(value, before, after, wy, out, low, high):
    empty = jnp.zeros((YK - YW, 2 * XC), F32)

    def pair(ref, z):
        return jnp.concatenate([ref[0, z], ref[0, z + 1]], axis=1)

    @pl.loop(0, ZC // 2, unroll=4)
    def _(b):
        z = 2 * b
        rows = jnp.concatenate([pair(before, z), pair(value, z), pair(after, z), empty], axis=0)
        hi, lo = split(rows)
        got = dot(wy[0], jnp.concatenate([hi, lo], axis=0))
        got = got[:YC] + got[32 : 32 + YC]
        out[0, z] = got[:, :XC]
        out[0, z + 1] = got[:, XC:]

    low[0] = out[0, :HALO]
    high[0] = out[0, ZC - HALO :]


def adjoint_y(g, value, before, after, wy):
    view = pl.BlockSpec((1, ZC, YC, XC), lambda v: (v, 0, 0, 0))
    edge = pl.BlockSpec((1, ZC, HALO, XC), lambda v: (v, 0, 0, 0))
    face = pl.BlockSpec((1, HALO, YC, XC), lambda v: (v, 0, 0, 0))
    face_shape = jax.ShapeDtypeStruct((GROUP, HALO, YC, XC), F32)
    return pl.pallas_call(
        adjoint_y_kernel,
        name="adjoint_y",
        grid=(GROUP,),
        out_shape=(jax.ShapeDtypeStruct((GROUP, ZC, YC, XC), F32), face_shape, face_shape),
        in_specs=[view, edge, edge, of_view(g, 64, 2 * YK)],
        out_specs=(view, face, face),
        **params(8),
    )(value, before, after, wy)


def pack_sides(first, last, q):
    group = lax.broadcasted_iota(jnp.int32, first.shape[1:], 1) // HALO
    acc = jnp.zeros(first.shape[1:], F32)
    for j in range(4):
        acc = jnp.where(group == j, pltpu.roll(first[4 * q + j], HALO * j + HALO, 1), acc)
        acc = jnp.where(group == 4 + j, pltpu.roll(last[4 * q + j], XC // 2 + HALO * j, 1), acc)
    return acc


def sides_kernel(first, last, out):
    for q in range(out.shape[0]):
        out[q] = pack_sides(first, last, q)


def pack(first, last):
    return pl.pallas_call(
        sides_kernel,
        name="sides",
        out_shape=jax.ShapeDtypeStruct((first.shape[0] // 4,) + first.shape[1:], F32),
        **params(1),
    )(first, last)


def add_logs(g, taps, value, before, after, win, total):
    win[:HALO] = before[0]
    win[HALO : HALO + ZC] = value[0]
    win[HALO + ZC :] = after[0]

    def store(z0, y0, back):
        total[pl.ds(z0, 16), y0 : y0 + 8, :] += jnp.log(back)

    z_sum(win, taps, g * GROUP + pl.program_id(0), True, store)


def first_logs_kernel(g, taps, value, before, after, total, win):
    @pl.when(pl.program_id(0) == 0)
    def _():
        total[...] = jnp.zeros_like(total)

    add_logs(g, taps, value, before, after, win, total)


def last_logs_kernel(g, taps, value, before, after, logs, estimate, out, sides, win, total):
    @pl.when(pl.program_id(0) == 0)
    def _():
        total[...] = logs[...]

    add_logs(g, taps, value, before, after, win, total)

    @pl.when(pl.program_id(0) == GROUP - 1)
    def _():
        out[...] = estimate[...] * jnp.exp(total[...] / VIEWS)

        @pl.loop(0, ZC // 4)
        def _(q):
            sides[q] = pack_sides(out, out, q)


def adjoint_z(g, taps, value, before, after, logs, estimate):
    view = pl.BlockSpec((1, ZC, YC, XC), lambda v: (v, 0, 0, 0))
    face = pl.BlockSpec((1, HALO, YC, XC), lambda v: (v, 0, 0, 0))
    chunk = pl.BlockSpec((ZC, YC, XC), lambda v: (0, 0, 0))
    packed = pl.BlockSpec((ZC // 4, YC, XC), lambda v: (0, 0, 0))
    chunk_shape = jax.ShapeDtypeStruct((ZC, YC, XC), F32)
    ins = [pl.BlockSpec(memory_space=pltpu.SMEM), view, face, face]
    win = pltpu.VMEM((ZW, YC, XC), F32)
    args = (taps, value, before, after)
    if logs is None:
        return pl.pallas_call(
            functools.partial(first_logs_kernel, g),
            name="first_logs",
            grid=(GROUP,),
            out_shape=chunk_shape,
            in_specs=ins,
            out_specs=chunk,
            scratch_shapes=[win],
            **params(9),
        )(*args)
    return pl.pallas_call(
        functools.partial(last_logs_kernel, g),
        name="last_logs",
        grid=(GROUP,),
        out_shape=(chunk_shape, jax.ShapeDtypeStruct((ZC // 4, YC, XC), F32)),
        in_specs=ins + [chunk, chunk],
        out_specs=(chunk, packed),
        scratch_shapes=[win, pltpu.VMEM((ZC, YC, XC), F32)],
        **params(10),
    )(*args, logs, estimate)


def gather_views(row):
    mine = jnp.arange(VIEWS)[:, None, None] == lax.axis_index(V)
    rows = jnp.where(mine, row[None], 0.0)
    for k in (1, 2, 4):
        rows = rows + lax.ppermute(rows, V, [(i, i ^ k) for i in range(VIEWS)])
    return rows


def add_z(blocks):
    before, after = exchange(blocks[0], blocks[SLABS - 1], "z", 4)
    return jnp.concatenate([before[None], blocks, after[None]], axis=0)


def first_window(slab):
    padded = jnp.pad(slab, ((0, 0), (HALO, HALO), (XC, XC)))
    c = lax.axis_index(V)
    before, own, after = (lax.dynamic_slice_in_dim(padded, XC * (c + k), XC, axis=2) for k in range(3))
    planes = jnp.concatenate([own, pack(before, after)], axis=0)
    me = lax.axis_index(S)

    def rows(k):
        return lax.dynamic_slice_in_dim(planes, YC * k, YW, axis=1)

    got = [rows(me)]
    for k in range(1, SLABS):
        got.append(lax.ppermute(rows(me ^ k), S, [(i, i ^ k) for i in range(SLABS)]))
    got = jnp.stack(got)
    blocks = jnp.stack([lax.dynamic_index_in_dim(got, me ^ k, 0, keepdims=False) for k in range(SLABS)])
    return add_z(blocks)


def next_window(chunk, sides):
    before, after = exchange(sides, sides, V, VIEWS)
    lane = lax.broadcasted_iota(jnp.int32, sides.shape, 2)
    packed = jnp.where(lane < XC // 2, before, after)
    blocks = [chunk.reshape(SLABS, DEPTH, YC, XC), packed.reshape(SLABS, PACKED, YC, XC)]
    blocks = add_z(jnp.concatenate(blocks, axis=1))
    before, after = exchange(blocks[:, :, :HALO], blocks[:, :, YC - HALO :], S, SLABS)
    return jnp.concatenate([before, blocks, after], axis=2)


def matrices_kernel(taps, fy, fx, fp, ax, side, ay):
    v = pl.program_id(0)

    def row_column(rows, columns):
        return tuple(lax.broadcasted_iota(jnp.int32, (rows, columns), d) for d in range(2))

    def stacked(ref, at, value):
        hi, lo = split(value)
        ref[at + (slice(0, XC), slice(0, XC))] = hi
        ref[at + (slice(0, XC), slice(XC, 2 * XC))] = lo
        ref[at + (slice(XC, 2 * XC), slice(0, XC))] = hi
        ref[at + (slice(XC, 2 * XC), slice(XC, 2 * XC))] = jnp.zeros_like(lo)

    def along_y(value):
        hi, lo = split(value)
        column = row_column(*value.shape)[1]
        return jnp.where(column < 2 * YK, hi.astype(F32), lo.astype(F32))

    r, c = row_column(XC, XC)
    stacked(fx, (0,), banded(taps, v, 0, r - c + RADIUS))
    stacked(ax, (0,), banded(taps, v, 0, c - r + RADIUS))
    x_of = jnp.where(r < XC // 2, r % HALO - HALO, r % HALO + XC)
    packed = banded(taps, v, 0, x_of - c + RADIUS)
    for j in range(4):
        stacked(fp, (0, j), jnp.where(r // HALO % 4 == j, packed, 0.0))
    before = banded(taps, v, 0, c - (r % HALO - HALO) + RADIUS)
    after = banded(taps, v, 0, c - (r % HALO + XC) + RADIUS)
    for half in range(2):
        value = jnp.where(r // HALO == GROUP * half + v % GROUP, before, 0.0)
        value = jnp.where(r // HALO == GROUP * (1 - half) + v % GROUP, after, value)
        stacked(side, (0, half), value)
    r, c = row_column(YC, 3 * YK)
    fy[...] = along_y(banded(taps, v, 1, c % YK - HALO - r + RADIUS))
    r, c = row_column(64, 2 * YK)
    hi, lo = split(banded(taps, v, 1, r % 32 - (c % YK - HALO) + RADIUS))
    value = jnp.where(r < 32, hi.astype(F32), jnp.where(c < YK, lo.astype(F32), 0.0))
    ay[0] = value.astype(BF16)


def matrices(taps):
    shapes = [
        (2 * XC, 2 * XC),
        (4, 2 * XC, 2 * XC),
        (2 * XC, 2 * XC),
        (2, 2 * XC, 2 * XC),
        (64, 2 * YK),
    ]
    fy, fx, fp, ax, side, ay = pl.pallas_call(
        matrices_kernel,
        name="matrices",
        grid=(VIEWS,),
        out_shape=[jax.ShapeDtypeStruct((VIEWS * YC, 3 * YK), F32)]
        + [jax.ShapeDtypeStruct((VIEWS,) + shape, BF16) for shape in shapes],
        in_specs=[pl.BlockSpec(memory_space=pltpu.SMEM)],
        out_specs=[pl.BlockSpec((YC, 3 * YK), lambda v: (v, 0))] + [of_view(0, *shape) for shape in shapes],
        **params(1),
    )(taps)
    return (fy, fx, fp), (ax, side), ay


def spread_kernel(got, out):
    for c in range(VIEWS):
        for y in range(SLABS):
            out[:, y * YC : (y + 1) * YC, c * XC : (c + 1) * XC] = got[c, y]


def spread(got):
    planes = 2
    return pl.pallas_call(
        spread_kernel,
        name="spread",
        grid=(DEPTH // planes,),
        out_shape=jax.ShapeDtypeStruct((DEPTH, SLABS * YC, VIEWS * XC), F32),
        in_specs=[pl.BlockSpec((VIEWS, SLABS, planes, YC, XC), lambda b: (0, 0, b, 0, 0))],
        out_specs=pl.BlockSpec((planes, SLABS * YC, VIEWS * XC), lambda b: (b, 0, 0)),
        **params(5),
    )(got)


def per_device(views_data, estimate, kernels):
    everyone = gather_views(kernels[0])
    blocks = views_data[0].reshape(DEPTH, SLABS, YC, VIEWS, XC).transpose(3, 1, 0, 2, 4)
    blocks = blocks.reshape(VIEWS * SLABS, DEPTH, YC, XC)
    blocks, everyone = lax.optimization_barrier((blocks, everyone))
    data = lax.all_to_all(blocks, V + S, 0, 0, tiled=True).reshape(VIEWS, ZC, YC, XC)
    taps = (everyone / jnp.sum(everyone, axis=-1, keepdims=True)).reshape(VIEWS, 3 * TAPS)
    w_forward, w_x, w_y = matrices(taps)
    window = first_window(estimate)
    chunk = window[1 : 1 + SLABS, :DEPTH, HALO : HALO + YC].reshape(ZC, YC, XC)
    groups = range(VIEWS // GROUP)
    for number in range(ITERS):
        if number:
            window = next_window(chunk, sides)
        if not number:
            blurred = [forward(g, taps, window, None, *w_forward) for g in groups]
        faces = []
        for g in groups:
            if number:
                ratio, left, right = forward(g, taps, window, data, *w_forward)
            else:
                ratio, left, right = divide_by(g, data, blurred[g])
            faces.append((ratio,) + exchange(left, right, V, VIEWS))
        edges = []
        for g in groups:
            value, top, bottom = adjoint_x(g, *faces[g], *w_x)
            edges.append((value,) + exchange(top, bottom, S, SLABS))
        ends = []
        for g in groups:
            value, low, high = adjoint_y(g, *edges[g], w_y)
            ends.append((value,) + exchange(low, high, "z", 4))
        logs = adjoint_z(0, taps, *ends[0], None, None)
        chunk, sides = adjoint_z(1, taps, *ends[1], logs, chunk)

    parts = chunk.reshape(1, SLABS, DEPTH, YC, XC)
    parts = jnp.broadcast_to(parts, (VIEWS, SLABS, DEPTH, YC, XC)).reshape(VIEWS * SLABS, DEPTH, YC, XC)
    got = lax.all_to_all(parts, V + S, 0, 0, tiled=True).reshape(VIEWS, SLABS, DEPTH, YC, XC)
    return spread(got)


def solution(mesh):
    fine = Mesh(mesh.devices.reshape(2, 4, 4, 2, 2), V + ("z",) + S)
    gz = ("z",) + S
    return jax.shard_map(
        per_device,
        mesh=fine,
        in_specs=(P(V, gz, None, None), P(gz, None, None), P(V, None, None)),
        out_specs=P(gz, None, None),
        check_vma=False,
    )
```

```python
import functools

import jax
import jax.numpy as jnp
from jax import lax
from jax.experimental import pallas as pl
from jax.experimental.pallas import tpu as pltpu
from jax.sharding import Mesh
from jax.sharding import PartitionSpec as P

TAPS = 31
ITERS = 2
RADIUS = 15
HALO = 16
VIEWS = 8
GROUP = 4
ZC = 64
YC = 24
XC = 128
YW = YC + 2 * HALO
YK = 64
ZW = ZC + 2 * HALO
SLABS = 4
DEPTH = ZC // SLABS
PACKED = DEPTH // 4
V = ("yh", "x")
S = ("yl", "co")
F32 = jnp.float32
BF16 = jnp.bfloat16
LIMIT = 56 * 1024 * 1024


def params(us):
    cost = pl.CostEstimate(flops=int(us * 1e9), bytes_accessed=int(us * 2e6), transcendentals=0)
    return dict(compiler_params=pltpu.CompilerParams(vmem_limit_bytes=LIMIT), cost_estimate=cost)


def split(value):
    hi = value.astype(BF16)
    return hi, (value - hi.astype(F32)).astype(BF16)


def dot(a, b):
    return jnp.dot(a, b, preferred_element_type=F32)


def banded(taps, v, axis, offsets):
    result = jnp.zeros(offsets.shape, F32)
    for t in range(TAPS):
        result = jnp.where(offsets == t, taps[v, axis * TAPS + t], result)
    return result


def exchange(low, high, axis, size):
    up = [(i, i + 1) for i in range(size - 1)]
    down = [(j, i) for i, j in up]
    return lax.ppermute(high, axis, up), lax.ppermute(low, axis, down)


def z_sum(win, taps, v, flipped, store):
    @pl.loop(0, ZC // 16)
    def _(b):
        z0 = pl.multiple_of(b * 16, 16)
        for y0 in range(0, YC, 8):
            acc = jnp.zeros((16, 8, XC), F32)
            for t in range(TAPS):
                tap = taps[v, 2 * TAPS + (TAPS - 1 - t if flipped else t)]
                acc = acc + tap * win[pl.ds(z0 + t + 1, 16), y0 : y0 + 8, :]
            store(z0, y0, acc)


def blur_planes(g, taps, est, wy, wown, wpack, yown, ypack, win):
    v = pl.program_id(0)

    @pl.when(v == 0)
    def _():
        empty = jnp.zeros((YK - YW, 2 * XC), F32)
        matrix = wy[...].astype(BF16)

        @pl.loop(0, SLABS + 2)
        def _(b):
            for i in range((DEPTH + PACKED) // 2):
                planes = jnp.concatenate([est[b, 2 * i], est[b, 2 * i + 1]], axis=1)
                hi, lo = split(jnp.concatenate([planes, empty], axis=0))
                got = dot(matrix, jnp.concatenate([hi, lo, hi], axis=0))
                if i < DEPTH // 2:
                    dest, first = yown, b * DEPTH * YC + 2 * i * YC
                else:
                    dest, first = ypack, b * PACKED * YC + 2 * (i - DEPTH // 2) * YC
                rows = pl.ds(pl.multiple_of(first, 16), 2 * YC)
                for u in range(GROUP):
                    one = got[u * YC : (u + 1) * YC]
                    hi, lo = split(jnp.concatenate([one[:, :XC], one[:, XC:]], axis=0))
                    dest[u, rows, :] = jnp.concatenate([hi, lo], axis=1)

    step = 12

    @pl.loop(0, ZW // 4 // step)
    def _(b):
        rows = pl.ds(pl.multiple_of(b * step * 4 * YC, 16), step * 4 * YC)
        two = dot(yown[v, rows, :], wown[0])
        own = (two[:, :XC] + two[:, XC:]).reshape(step, 4, YC, XC)
        packed = ypack[v, pl.ds(pl.multiple_of(b * step * YC, 16), step * YC), :]
        for j in range(4):
            two = dot(packed, wpack[0, j])
            out = own[:, j] + (two[:, :XC] + two[:, XC:]).reshape(step, YC, XC)
            for q in range(step):
                win[b * step * 4 + q * 4 + j] = out[q]


def divide(z0, y0, recorded, blurred, ratio, left, right):
    v = pl.program_id(0)
    zs, ys = pl.ds(z0, 16), pl.ds(y0, 8)
    value = recorded[0, zs, ys, :] / blurred
    ratio[0, zs, ys, :] = value
    half = z0 // (ZC // 2)
    slot = lax.broadcasted_iota(jnp.int32, value.shape, 2) // HALO
    zs = pl.ds(z0 - half * (ZC // 2), 16)
    at = GROUP * (1 - half) + v
    first = pltpu.roll(value, HALO * at, 2)
    left[zs, ys, :] = jnp.where(slot == at, first, left[zs, ys, :])
    at = GROUP * half + v
    last = pltpu.roll(value, lax.rem(HALO * at + HALO, XC), 2)
    right[zs, ys, :] = jnp.where(slot == at, last, right[zs, ys, :])


def blur_kernel(g, taps, est, wy, wown, wpack, blurred, yown, ypack, win):
    blur_planes(g, taps, est, wy, wown, wpack, yown, ypack, win)

    def store(z0, y0, value):
        blurred[0, pl.ds(z0, 16), y0 : y0 + 8, :] = value

    z_sum(win, taps, g * GROUP + pl.program_id(0), False, store)


def blur_and_divide_kernel(g, taps, est, wy, wown, wpack, data, ratio, left, right, yown, ypack, win):
    blur_planes(g, taps, est, wy, wown, wpack, yown, ypack, win)

    def store(z0, y0, value):
        divide(z0, y0, data, value, ratio, left, right)

    z_sum(win, taps, g * GROUP + pl.program_id(0), False, store)


def divide_kernel(data, blurred, ratio, left, right):
    @pl.loop(0, ZC // 16)
    def _(b):
        z0 = pl.multiple_of(b * 16, 16)
        for y0 in range(0, YC, 8):
            divide(z0, y0, data, blurred[0, pl.ds(z0, 16), y0 : y0 + 8, :], ratio, left, right)


def of_view(g, *shape):
    return pl.BlockSpec((1,) + shape, lambda v: (v + g * GROUP,) + (0,) * len(shape))


OUT_VIEW = pl.BlockSpec((1, ZC, YC, XC), lambda v: (v, 0, 0, 0))
OUT_SIDES = pl.BlockSpec((ZC // 2, YC, XC), lambda v: (0, 0, 0))
VIEW_SHAPE = jax.ShapeDtypeStruct((GROUP, ZC, YC, XC), F32)
SIDES_SHAPE = jax.ShapeDtypeStruct((ZC // 2, YC, XC), F32)


def forward(g, taps, window, data, wy, wown, wpack):
    ins = [
        pl.BlockSpec(memory_space=pltpu.SMEM),
        pl.BlockSpec(window.shape, lambda v: (0, 0, 0, 0), pipeline_mode=pl.Buffered(1)),
        pl.BlockSpec((GROUP * YC, 3 * YK), lambda v: (g, 0), pipeline_mode=pl.Buffered(1)),
        of_view(g, 2 * XC, 2 * XC),
        of_view(g, 4, 2 * XC, 2 * XC),
    ]
    scratch = [
        pltpu.VMEM((GROUP, ZW * YC, 2 * XC), BF16),
        pltpu.VMEM((GROUP, ZW // 4 * YC, 2 * XC), BF16),
        pltpu.VMEM((ZW, YC, XC), F32),
    ]
    if data is None:
        return pl.pallas_call(
            functools.partial(blur_kernel, g),
            name="blur",
            grid=(GROUP,),
            out_shape=VIEW_SHAPE,
            in_specs=ins,
            out_specs=OUT_VIEW,
            scratch_shapes=scratch,
            **params(18),
        )(taps, window, wy, wown, wpack)
    return pl.pallas_call(
        functools.partial(blur_and_divide_kernel, g),
        name="blur_and_divide",
        grid=(GROUP,),
        out_shape=(VIEW_SHAPE, SIDES_SHAPE, SIDES_SHAPE),
        in_specs=ins + [of_view(g, ZC, YC, XC)],
        out_specs=(OUT_VIEW, OUT_SIDES, OUT_SIDES),
        scratch_shapes=scratch,
        **params(24),
    )(taps, window, wy, wown, wpack, data)


def divide_by(g, data, blurred):
    return pl.pallas_call(
        divide_kernel,
        name="divide",
        grid=(GROUP,),
        out_shape=(VIEW_SHAPE, SIDES_SHAPE, SIDES_SHAPE),
        in_specs=[of_view(g, ZC, YC, XC), OUT_VIEW],
        out_specs=(OUT_VIEW, OUT_SIDES, OUT_SIDES),
        **params(5),
    )(data, blurred)


def adjoint_x_kernel(ratio, before, after, wown, wside, out, top, bottom):
    planes = ZC // 2
    low_lanes = lax.broadcasted_iota(jnp.int32, (planes * YC, XC), 1) < XC // 2

    @pl.loop(0, 2)
    def _(half):
        rows = planes * YC
        zs = pl.ds(pl.multiple_of(half * planes, planes), planes)
        hi, lo = split(ratio[0, zs].reshape(rows, XC))
        is_before = low_lanes == (half == 0)
        shi, slo = split(jnp.where(is_before, before[...].reshape(rows, XC), after[...].reshape(rows, XC)))
        two = dot(jnp.concatenate([hi, lo], axis=1), wown[0])
        two = two + dot(jnp.concatenate([shi, slo], axis=1), wside[0, half])
        value = two[:, :XC] + two[:, XC:]
        value = value.reshape(planes, YC, XC)
        out[0, zs] = value
        top[0, zs] = value[:, :HALO]
        bottom[0, zs] = value[:, YC - HALO :]


def adjoint_x(g, ratio, before, after, wown, wside):
    view = pl.BlockSpec((1, ZC, YC, XC), lambda v: (v, 0, 0, 0))
    pack = pl.BlockSpec((ZC // 2, YC, XC), lambda v: (0, 0, 0))
    edge = pl.BlockSpec((1, ZC, HALO, XC), lambda v: (v, 0, 0, 0))
    edge_shape = jax.ShapeDtypeStruct((GROUP, ZC, HALO, XC), F32)
    return pl.pallas_call(
        adjoint_x_kernel,
        name="adjoint_x",
        grid=(GROUP,),
        out_shape=(jax.ShapeDtypeStruct((GROUP, ZC, YC, XC), F32), edge_shape, edge_shape),
        in_specs=[
            view,
            pack,
            pack,
            pl.BlockSpec((1, 2 * XC, 2 * XC), lambda v: (v + g * GROUP, 0, 0)),
            pl.BlockSpec((1, 2, 2 * XC, 2 * XC), lambda v: (v + g * GROUP, 0, 0, 0)),
        ],
        out_specs=(view, edge, edge),
        **params(8),
    )(ratio, before, after, wown, wside)


def adjoint_y_kernel(value, before, after, wy, out, low, high):
    empty = jnp.zeros((YK - YW, 2 * XC), F32)

    def pair(ref, z):
        return jnp.concatenate([ref[0, z], ref[0, z + 1]], axis=1)

    @pl.loop(0, ZC // 2, unroll=4)
    def _(b):
        z = 2 * b
        rows = jnp.concatenate([pair(before, z), pair(value, z), pair(after, z), empty], axis=0)
        hi, lo = split(rows)
        got = dot(wy[0], jnp.concatenate([hi, lo], axis=0))
        got = got[:YC] + got[32 : 32 + YC]
        out[0, z] = got[:, :XC]
        out[0, z + 1] = got[:, XC:]

    low[0] = out[0, :HALO]
    high[0] = out[0, ZC - HALO :]


def adjoint_y(g, value, before, after, wy):
    view = pl.BlockSpec((1, ZC, YC, XC), lambda v: (v, 0, 0, 0))
    edge = pl.BlockSpec((1, ZC, HALO, XC), lambda v: (v, 0, 0, 0))
    face = pl.BlockSpec((1, HALO, YC, XC), lambda v: (v, 0, 0, 0))
    face_shape = jax.ShapeDtypeStruct((GROUP, HALO, YC, XC), F32)
    return pl.pallas_call(
        adjoint_y_kernel,
        name="adjoint_y",
        grid=(GROUP,),
        out_shape=(jax.ShapeDtypeStruct((GROUP, ZC, YC, XC), F32), face_shape, face_shape),
        in_specs=[view, edge, edge, of_view(g, 64, 2 * YK)],
        out_specs=(view, face, face),
        **params(8),
    )(value, before, after, wy)


def pack_sides(first, last, q):
    group = lax.broadcasted_iota(jnp.int32, first.shape[1:], 1) // HALO
    acc = jnp.zeros(first.shape[1:], F32)
    for j in range(4):
        acc = jnp.where(group == j, pltpu.roll(first[4 * q + j], HALO * j + HALO, 1), acc)
        acc = jnp.where(group == 4 + j, pltpu.roll(last[4 * q + j], XC // 2 + HALO * j, 1), acc)
    return acc


def sides_kernel(first, last, out):
    for q in range(out.shape[0]):
        out[q] = pack_sides(first, last, q)


def pack(first, last):
    return pl.pallas_call(
        sides_kernel,
        name="sides",
        out_shape=jax.ShapeDtypeStruct((first.shape[0] // 4,) + first.shape[1:], F32),
        **params(1),
    )(first, last)


def add_logs(g, taps, value, before, after, win, total):
    win[:HALO] = before[0]
    win[HALO : HALO + ZC] = value[0]
    win[HALO + ZC :] = after[0]

    def store(z0, y0, back):
        total[pl.ds(z0, 16), y0 : y0 + 8, :] += jnp.log(back)

    z_sum(win, taps, g * GROUP + pl.program_id(0), True, store)


def first_logs_kernel(g, taps, value, before, after, total, win):
    @pl.when(pl.program_id(0) == 0)
    def _():
        total[...] = jnp.zeros_like(total)

    add_logs(g, taps, value, before, after, win, total)


def last_logs_kernel(g, taps, value, before, after, logs, estimate, out, sides, win, total):
    @pl.when(pl.program_id(0) == 0)
    def _():
        total[...] = logs[...]

    add_logs(g, taps, value, before, after, win, total)

    @pl.when(pl.program_id(0) == GROUP - 1)
    def _():
        out[...] = estimate[...] * jnp.exp(total[...] / VIEWS)

        @pl.loop(0, ZC // 4)
        def _(q):
            sides[q] = pack_sides(out, out, q)


def adjoint_z(g, taps, value, before, after, logs, estimate):
    view = pl.BlockSpec((1, ZC, YC, XC), lambda v: (v, 0, 0, 0))
    face = pl.BlockSpec((1, HALO, YC, XC), lambda v: (v, 0, 0, 0))
    chunk = pl.BlockSpec((ZC, YC, XC), lambda v: (0, 0, 0))
    packed = pl.BlockSpec((ZC // 4, YC, XC), lambda v: (0, 0, 0))
    chunk_shape = jax.ShapeDtypeStruct((ZC, YC, XC), F32)
    ins = [pl.BlockSpec(memory_space=pltpu.SMEM), view, face, face]
    win = pltpu.VMEM((ZW, YC, XC), F32)
    args = (taps, value, before, after)
    if logs is None:
        return pl.pallas_call(
            functools.partial(first_logs_kernel, g),
            name="first_logs",
            grid=(GROUP,),
            out_shape=chunk_shape,
            in_specs=ins,
            out_specs=chunk,
            scratch_shapes=[win],
            **params(9),
        )(*args)
    return pl.pallas_call(
        functools.partial(last_logs_kernel, g),
        name="last_logs",
        grid=(GROUP,),
        out_shape=(chunk_shape, jax.ShapeDtypeStruct((ZC // 4, YC, XC), F32)),
        in_specs=ins + [chunk, chunk],
        out_specs=(chunk, packed),
        scratch_shapes=[win, pltpu.VMEM((ZC, YC, XC), F32)],
        **params(10),
    )(*args, logs, estimate)


def gather_views(row):
    mine = jnp.arange(VIEWS)[:, None, None] == lax.axis_index(V)
    rows = jnp.where(mine, row[None], 0.0)
    for k in (1, 2, 4):
        rows = rows + lax.ppermute(rows, V, [(i, i ^ k) for i in range(VIEWS)])
    return rows


def add_z(blocks):
    before, after = exchange(blocks[0], blocks[SLABS - 1], "z", 4)
    return jnp.concatenate([before[None], blocks, after[None]], axis=0)


def first_columns(slab):
    padded = jnp.pad(slab, ((0, 0), (HALO, HALO), (XC, XC)))
    c = lax.axis_index(V)
    before, own, after = (lax.dynamic_slice_in_dim(padded, XC * (c + k), XC, axis=2) for k in range(3))
    return jnp.concatenate([own, pack(before, after)], axis=0)


def first_window(planes, matrix):
    me = lax.axis_index(S)

    def rows(k):
        return lax.dynamic_slice_in_dim(planes, YC * k, YW, axis=1)

    got = [rows(me)]
    for k in range(1, SLABS):
        got.append(lax.ppermute(rows(me ^ k), S, [(i, i ^ k) for i in range(SLABS)]))
    *got, _ = lax.optimization_barrier((*got, matrix))
    got = jnp.stack(got)
    blocks = jnp.stack([lax.dynamic_index_in_dim(got, me ^ k, 0, keepdims=False) for k in range(SLABS)])
    return add_z(blocks)


def next_window(chunk, sides):
    before, after = exchange(sides, sides, V, VIEWS)
    lane = lax.broadcasted_iota(jnp.int32, sides.shape, 2)
    packed = jnp.where(lane < XC // 2, before, after)
    blocks = [chunk.reshape(SLABS, DEPTH, YC, XC), packed.reshape(SLABS, PACKED, YC, XC)]
    blocks = add_z(jnp.concatenate(blocks, axis=1))
    before, after = exchange(blocks[:, :, :HALO], blocks[:, :, YC - HALO :], S, SLABS)
    return jnp.concatenate([before, blocks, after], axis=2)


def matrices_kernel(taps, fy, fx, fp, ax, side, ay):
    v = pl.program_id(0)

    def row_column(rows, columns):
        return tuple(lax.broadcasted_iota(jnp.int32, (rows, columns), d) for d in range(2))

    def stacked(ref, at, value):
        hi, lo = split(value)
        ref[at + (slice(0, XC), slice(0, XC))] = hi
        ref[at + (slice(0, XC), slice(XC, 2 * XC))] = lo
        ref[at + (slice(XC, 2 * XC), slice(0, XC))] = hi
        ref[at + (slice(XC, 2 * XC), slice(XC, 2 * XC))] = jnp.zeros_like(lo)

    def along_y(value):
        hi, lo = split(value)
        column = row_column(*value.shape)[1]
        return jnp.where(column < 2 * YK, hi.astype(F32), lo.astype(F32))

    r, c = row_column(XC, XC)
    stacked(fx, (0,), banded(taps, v, 0, r - c + RADIUS))
    stacked(ax, (0,), banded(taps, v, 0, c - r + RADIUS))
    x_of = jnp.where(r < XC // 2, r % HALO - HALO, r % HALO + XC)
    packed = banded(taps, v, 0, x_of - c + RADIUS)
    for j in range(4):
        stacked(fp, (0, j), jnp.where(r // HALO % 4 == j, packed, 0.0))
    before = banded(taps, v, 0, c - (r % HALO - HALO) + RADIUS)
    after = banded(taps, v, 0, c - (r % HALO + XC) + RADIUS)
    for half in range(2):
        value = jnp.where(r // HALO == GROUP * half + v % GROUP, before, 0.0)
        value = jnp.where(r // HALO == GROUP * (1 - half) + v % GROUP, after, value)
        stacked(side, (0, half), value)
    r, c = row_column(YC, 3 * YK)
    fy[...] = along_y(banded(taps, v, 1, c % YK - HALO - r + RADIUS))
    r, c = row_column(64, 2 * YK)
    hi, lo = split(banded(taps, v, 1, r % 32 - (c % YK - HALO) + RADIUS))
    value = jnp.where(r < 32, hi.astype(F32), jnp.where(c < YK, lo.astype(F32), 0.0))
    ay[0] = value.astype(BF16)


def matrices(taps):
    shapes = [
        (2 * XC, 2 * XC),
        (4, 2 * XC, 2 * XC),
        (2 * XC, 2 * XC),
        (2, 2 * XC, 2 * XC),
        (64, 2 * YK),
    ]
    fy, fx, fp, ax, side, ay = pl.pallas_call(
        matrices_kernel,
        name="matrices",
        grid=(VIEWS,),
        out_shape=[jax.ShapeDtypeStruct((VIEWS * YC, 3 * YK), F32)]
        + [jax.ShapeDtypeStruct((VIEWS,) + shape, BF16) for shape in shapes],
        in_specs=[pl.BlockSpec(memory_space=pltpu.SMEM)],
        out_specs=[pl.BlockSpec((YC, 3 * YK), lambda v: (v, 0))] + [of_view(0, *shape) for shape in shapes],
        **params(10),
    )(taps)
    return (fy, fx, fp), (ax, side), ay


def spread_kernel(got, out):
    for c in range(VIEWS):
        for y in range(SLABS):
            out[:, y * YC : (y + 1) * YC, c * XC : (c + 1) * XC] = got[c, y]


def spread(got):
    planes = 2
    return pl.pallas_call(
        spread_kernel,
        name="spread",
        grid=(DEPTH // planes,),
        out_shape=jax.ShapeDtypeStruct((DEPTH, SLABS * YC, VIEWS * XC), F32),
        in_specs=[pl.BlockSpec((VIEWS, SLABS, planes, YC, XC), lambda b: (0, 0, b, 0, 0))],
        out_specs=pl.BlockSpec((planes, SLABS * YC, VIEWS * XC), lambda b: (b, 0, 0)),
        **params(5),
    )(got)


def per_device(views_data, estimate, kernels):
    everyone = gather_views(kernels[0])
    blocks = views_data[0].reshape(DEPTH, SLABS, YC, VIEWS, XC).transpose(3, 1, 0, 2, 4)
    blocks = blocks.reshape(VIEWS * SLABS, DEPTH, YC, XC)
    planes = first_columns(estimate)
    blocks, planes, everyone = lax.optimization_barrier((blocks, planes, everyone))
    data = lax.all_to_all(blocks, V + S, 0, 0, tiled=True).reshape(VIEWS, ZC, YC, XC)
    taps = (everyone / jnp.sum(everyone, axis=-1, keepdims=True)).reshape(VIEWS, 3 * TAPS)
    w_forward, w_x, w_y = matrices(taps)
    window = first_window(planes, w_y)
    chunk = window[1 : 1 + SLABS, :DEPTH, HALO : HALO + YC].reshape(ZC, YC, XC)
    groups = range(VIEWS // GROUP)
    for number in range(ITERS):
        if number:
            window = next_window(chunk, sides)
        if not number:
            blurred = [forward(g, taps, window, None, *w_forward) for g in groups]
        faces = []
        for g in groups:
            if number:
                ratio, left, right = forward(g, taps, window, data, *w_forward)
            else:
                ratio, left, right = divide_by(g, data, blurred[g])
            faces.append((ratio,) + exchange(left, right, V, VIEWS))
        edges = []
        for g in groups:
            value, top, bottom = adjoint_x(g, *faces[g], *w_x)
            edges.append((value,) + exchange(top, bottom, S, SLABS))
        ends = []
        for g in groups:
            value, low, high = adjoint_y(g, *edges[g], w_y)
            ends.append((value,) + exchange(low, high, "z", 4))
        logs = adjoint_z(0, taps, *ends[0], None, None)
        chunk, sides = adjoint_z(1, taps, *ends[1], logs, chunk)

    parts = chunk.reshape(1, SLABS, DEPTH, YC, XC)
    parts = jnp.broadcast_to(parts, (VIEWS, SLABS, DEPTH, YC, XC)).reshape(VIEWS * SLABS, DEPTH, YC, XC)
    got = lax.all_to_all(parts, V + S, 0, 0, tiled=True).reshape(VIEWS, SLABS, DEPTH, YC, XC)
    return spread(got)


def solution(mesh):
    fine = Mesh(mesh.devices.reshape(2, 4, 4, 2, 2), V + ("z",) + S)
    gz = ("z",) + S
    return jax.shard_map(
        per_device,
        mesh=fine,
        in_specs=(P(V, gz, None, None), P(gz, None, None), P(V, None, None)),
        out_specs=P(gz, None, None),
        check_vma=False,
    )
```

```python
import functools

import jax
import jax.numpy as jnp
from jax import lax
from jax.experimental import pallas as pl
from jax.experimental.pallas import tpu as pltpu
from jax.sharding import Mesh
from jax.sharding import PartitionSpec as P

TAPS = 31
ITERS = 2
RADIUS = 15
HALO = 16
VIEWS = 8
GROUP = 4
ZC = 64
YC = 24
XC = 128
YW = YC + 2 * HALO
YK = 64
ZW = ZC + 2 * HALO
SLABS = 4
DEPTH = ZC // SLABS
PACKED = DEPTH // 4
V = ("yh", "x")
S = ("yl", "co")
F32 = jnp.float32
BF16 = jnp.bfloat16
MIB = 1024 * 1024


def params(us, mib):
    cost = pl.CostEstimate(flops=int(us * 1e9), bytes_accessed=int(us * 2e6), transcendentals=0)
    return dict(compiler_params=pltpu.CompilerParams(vmem_limit_bytes=mib * MIB), cost_estimate=cost)


def split(value):
    hi = value.astype(BF16)
    return hi, (value - hi.astype(F32)).astype(BF16)


def dot(a, b):
    return jnp.dot(a, b, preferred_element_type=F32)


def banded(taps, v, axis, offsets):
    result = jnp.zeros(offsets.shape, F32)
    for t in range(TAPS):
        result = jnp.where(offsets == t, taps[v, axis * TAPS + t], result)
    return result


def exchange(low, high, axis, size):
    up = [(i, i + 1) for i in range(size - 1)]
    down = [(j, i) for i, j in up]
    return lax.ppermute(high, axis, up), lax.ppermute(low, axis, down)


def z_sum(win, taps, v, flipped, store):
    @pl.loop(0, ZC // 16)
    def _(b):
        z0 = pl.multiple_of(b * 16, 16)
        for y0 in range(0, YC, 8):
            acc = jnp.zeros((16, 8, XC), F32)
            for t in range(TAPS):
                tap = taps[v, 2 * TAPS + (TAPS - 1 - t if flipped else t)]
                acc = acc + tap * win[pl.ds(z0 + t + 1, 16), y0 : y0 + 8, :]
            store(z0, y0, acc)


def blur_planes(g, taps, est, wy, wown, wpack, yown, ypack, win):
    v = pl.program_id(0)

    @pl.when(v == 0)
    def _():
        empty = jnp.zeros((YK - YW, 2 * XC), F32)
        matrix = wy[...].astype(BF16)

        @pl.loop(0, SLABS + 2)
        def _(b):
            for i in range((DEPTH + PACKED) // 2):
                planes = jnp.concatenate([est[b, 2 * i], est[b, 2 * i + 1]], axis=1)
                hi, lo = split(jnp.concatenate([planes, empty], axis=0))
                got = dot(matrix, jnp.concatenate([hi, lo, hi], axis=0))
                if i < DEPTH // 2:
                    dest, first = yown, b * DEPTH * YC + 2 * i * YC
                else:
                    dest, first = ypack, b * PACKED * YC + 2 * (i - DEPTH // 2) * YC
                rows = pl.ds(pl.multiple_of(first, 16), 2 * YC)
                for u in range(GROUP):
                    one = got[u * YC : (u + 1) * YC]
                    hi, lo = split(jnp.concatenate([one[:, :XC], one[:, XC:]], axis=0))
                    dest[u, rows, :] = jnp.concatenate([hi, lo], axis=1)

    step = 12

    @pl.loop(0, ZW // 4 // step)
    def _(b):
        rows = pl.ds(pl.multiple_of(b * step * 4 * YC, 16), step * 4 * YC)
        two = dot(yown[v, rows, :], wown[0])
        own = (two[:, :XC] + two[:, XC:]).reshape(step, 4, YC, XC)
        packed = ypack[v, pl.ds(pl.multiple_of(b * step * YC, 16), step * YC), :]
        for j in range(4):
            two = dot(packed, wpack[0, j])
            out = own[:, j] + (two[:, :XC] + two[:, XC:]).reshape(step, YC, XC)
            for q in range(step):
                win[b * step * 4 + q * 4 + j] = out[q]


def divide(z0, y0, recorded, blurred, ratio, left, right):
    v = pl.program_id(0)
    zs, ys = pl.ds(z0, 16), pl.ds(y0, 8)
    value = recorded[0, zs, ys, :] / blurred
    ratio[0, zs, ys, :] = value
    half = z0 // (ZC // 2)
    slot = lax.broadcasted_iota(jnp.int32, value.shape, 2) // HALO
    zs = pl.ds(z0 - half * (ZC // 2), 16)
    at = GROUP * (1 - half) + v
    first = pltpu.roll(value, HALO * at, 2)
    left[zs, ys, :] = jnp.where(slot == at, first, left[zs, ys, :])
    at = GROUP * half + v
    last = pltpu.roll(value, lax.rem(HALO * at + HALO, XC), 2)
    right[zs, ys, :] = jnp.where(slot == at, last, right[zs, ys, :])


def blur_kernel(g, taps, est, wy, wown, wpack, blurred, yown, ypack, win):
    blur_planes(g, taps, est, wy, wown, wpack, yown, ypack, win)

    def store(z0, y0, value):
        blurred[0, pl.ds(z0, 16), y0 : y0 + 8, :] = value

    z_sum(win, taps, g * GROUP + pl.program_id(0), False, store)


def blur_and_divide_kernel(g, taps, est, wy, wown, wpack, data, ratio, left, right, yown, ypack, win):
    blur_planes(g, taps, est, wy, wown, wpack, yown, ypack, win)

    def store(z0, y0, value):
        divide(z0, y0, data, value, ratio, left, right)

    z_sum(win, taps, g * GROUP + pl.program_id(0), False, store)


def divide_kernel(data, blurred, ratio, left, right):
    @pl.loop(0, ZC // 16)
    def _(b):
        z0 = pl.multiple_of(b * 16, 16)
        for y0 in range(0, YC, 8):
            divide(z0, y0, data, blurred[0, pl.ds(z0, 16), y0 : y0 + 8, :], ratio, left, right)


def of_view(g, *shape):
    return pl.BlockSpec((1,) + shape, lambda v: (v + g * GROUP,) + (0,) * len(shape))


OUT_VIEW = pl.BlockSpec((1, ZC, YC, XC), lambda v: (v, 0, 0, 0))
OUT_SIDES = pl.BlockSpec((ZC // 2, YC, XC), lambda v: (0, 0, 0))
VIEW_SHAPE = jax.ShapeDtypeStruct((GROUP, ZC, YC, XC), F32)
SIDES_SHAPE = jax.ShapeDtypeStruct((ZC // 2, YC, XC), F32)


def forward(g, taps, window, data, wy, wown, wpack):
    ins = [
        pl.BlockSpec(memory_space=pltpu.SMEM),
        pl.BlockSpec(window.shape, lambda v: (0, 0, 0, 0), pipeline_mode=pl.Buffered(1)),
        pl.BlockSpec((GROUP * YC, 3 * YK), lambda v: (g, 0), pipeline_mode=pl.Buffered(1)),
        of_view(g, 2 * XC, 2 * XC),
        of_view(g, 4, 2 * XC, 2 * XC),
    ]
    scratch = [
        pltpu.VMEM((GROUP, ZW * YC, 2 * XC), BF16),
        pltpu.VMEM((GROUP, ZW // 4 * YC, 2 * XC), BF16),
        pltpu.VMEM((ZW, YC, XC), F32),
    ]
    if data is None:
        return pl.pallas_call(
            functools.partial(blur_kernel, g),
            name="blur",
            grid=(GROUP,),
            out_shape=VIEW_SHAPE,
            in_specs=ins,
            out_specs=OUT_VIEW,
            scratch_shapes=scratch,
            **params(18, 32),
        )(taps, window, wy, wown, wpack)
    return pl.pallas_call(
        functools.partial(blur_and_divide_kernel, g),
        name="blur_and_divide",
        grid=(GROUP,),
        out_shape=(VIEW_SHAPE, SIDES_SHAPE, SIDES_SHAPE),
        in_specs=ins + [of_view(g, ZC, YC, XC)],
        out_specs=(OUT_VIEW, OUT_SIDES, OUT_SIDES),
        scratch_shapes=scratch,
        **params(24, 32),
    )(taps, window, wy, wown, wpack, data)


def divide_by(g, data, blurred):
    return pl.pallas_call(
        divide_kernel,
        name="divide",
        grid=(GROUP,),
        out_shape=(VIEW_SHAPE, SIDES_SHAPE, SIDES_SHAPE),
        in_specs=[of_view(g, ZC, YC, XC), OUT_VIEW],
        out_specs=(OUT_VIEW, OUT_SIDES, OUT_SIDES),
        **params(5, 16),
    )(data, blurred)


def adjoint_x_kernel(ratio, before, after, wown, wside, out, top, bottom):
    planes = ZC // 2
    low_lanes = lax.broadcasted_iota(jnp.int32, (planes * YC, XC), 1) < XC // 2

    @pl.loop(0, 2)
    def _(half):
        rows = planes * YC
        zs = pl.ds(pl.multiple_of(half * planes, planes), planes)
        hi, lo = split(ratio[0, zs].reshape(rows, XC))
        is_before = low_lanes == (half == 0)
        shi, slo = split(jnp.where(is_before, before[...].reshape(rows, XC), after[...].reshape(rows, XC)))
        two = dot(jnp.concatenate([hi, lo], axis=1), wown[0])
        two = two + dot(jnp.concatenate([shi, slo], axis=1), wside[0, half])
        value = two[:, :XC] + two[:, XC:]
        value = value.reshape(planes, YC, XC)
        out[0, zs] = value
        top[0, zs] = value[:, :HALO]
        bottom[0, zs] = value[:, YC - HALO :]


def adjoint_x(g, ratio, before, after, wown, wside):
    view = pl.BlockSpec((1, ZC, YC, XC), lambda v: (v, 0, 0, 0))
    pack = pl.BlockSpec((ZC // 2, YC, XC), lambda v: (0, 0, 0))
    edge = pl.BlockSpec((1, ZC, HALO, XC), lambda v: (v, 0, 0, 0))
    edge_shape = jax.ShapeDtypeStruct((GROUP, ZC, HALO, XC), F32)
    return pl.pallas_call(
        adjoint_x_kernel,
        name="adjoint_x",
        grid=(GROUP,),
        out_shape=(jax.ShapeDtypeStruct((GROUP, ZC, YC, XC), F32), edge_shape, edge_shape),
        in_specs=[
            view,
            pack,
            pack,
            pl.BlockSpec((1, 2 * XC, 2 * XC), lambda v: (v + g * GROUP, 0, 0)),
            pl.BlockSpec((1, 2, 2 * XC, 2 * XC), lambda v: (v + g * GROUP, 0, 0, 0)),
        ],
        out_specs=(view, edge, edge),
        **params(8, 20),
    )(ratio, before, after, wown, wside)


def adjoint_y_kernel(value, before, after, wy, out, low, high):
    empty = jnp.zeros((YK - YW, 2 * XC), F32)

    def pair(ref, z):
        return jnp.concatenate([ref[0, z], ref[0, z + 1]], axis=1)

    @pl.loop(0, ZC // 2, unroll=4)
    def _(b):
        z = 2 * b
        rows = jnp.concatenate([pair(before, z), pair(value, z), pair(after, z), empty], axis=0)
        hi, lo = split(rows)
        got = dot(wy[0], jnp.concatenate([hi, lo], axis=0))
        got = got[:YC] + got[32 : 32 + YC]
        out[0, z] = got[:, :XC]
        out[0, z + 1] = got[:, XC:]

    low[0] = out[0, :HALO]
    high[0] = out[0, ZC - HALO :]


def adjoint_y(g, value, before, after, wy):
    view = pl.BlockSpec((1, ZC, YC, XC), lambda v: (v, 0, 0, 0))
    edge = pl.BlockSpec((1, ZC, HALO, XC), lambda v: (v, 0, 0, 0))
    face = pl.BlockSpec((1, HALO, YC, XC), lambda v: (v, 0, 0, 0))
    face_shape = jax.ShapeDtypeStruct((GROUP, HALO, YC, XC), F32)
    return pl.pallas_call(
        adjoint_y_kernel,
        name="adjoint_y",
        grid=(GROUP,),
        out_shape=(jax.ShapeDtypeStruct((GROUP, ZC, YC, XC), F32), face_shape, face_shape),
        in_specs=[view, edge, edge, of_view(g, 64, 2 * YK)],
        out_specs=(view, face, face),
        **params(8, 16),
    )(value, before, after, wy)


def pack_sides(first, last, q):
    group = lax.broadcasted_iota(jnp.int32, first.shape[1:], 1) // HALO
    acc = jnp.zeros(first.shape[1:], F32)
    for j in range(4):
        acc = jnp.where(group == j, pltpu.roll(first[4 * q + j], HALO * j + HALO, 1), acc)
        acc = jnp.where(group == 4 + j, pltpu.roll(last[4 * q + j], XC // 2 + HALO * j, 1), acc)
    return acc


def sides_kernel(first, last, out):
    for q in range(out.shape[0]):
        out[q] = pack_sides(first, last, q)


def pack(first, last):
    return pl.pallas_call(
        sides_kernel,
        name="sides",
        out_shape=jax.ShapeDtypeStruct((first.shape[0] // 4,) + first.shape[1:], F32),
        **params(1, 16),
    )(first, last)


def add_logs(g, taps, value, before, after, win, total):
    win[:HALO] = before[0]
    win[HALO : HALO + ZC] = value[0]
    win[HALO + ZC :] = after[0]

    def store(z0, y0, back):
        total[pl.ds(z0, 16), y0 : y0 + 8, :] += jnp.log(back)

    z_sum(win, taps, g * GROUP + pl.program_id(0), True, store)


def first_logs_kernel(g, taps, value, before, after, total, win):
    @pl.when(pl.program_id(0) == 0)
    def _():
        total[...] = jnp.zeros_like(total)

    add_logs(g, taps, value, before, after, win, total)


def last_logs_kernel(g, taps, value, before, after, logs, estimate, out, sides, win, total):
    @pl.when(pl.program_id(0) == 0)
    def _():
        total[...] = logs[...]

    add_logs(g, taps, value, before, after, win, total)

    @pl.when(pl.program_id(0) == GROUP - 1)
    def _():
        out[...] = estimate[...] * jnp.exp(total[...] / VIEWS)

        @pl.loop(0, ZC // 4)
        def _(q):
            sides[q] = pack_sides(out, out, q)


def adjoint_z(g, taps, value, before, after, logs, estimate):
    view = pl.BlockSpec((1, ZC, YC, XC), lambda v: (v, 0, 0, 0))
    face = pl.BlockSpec((1, HALO, YC, XC), lambda v: (v, 0, 0, 0))
    chunk = pl.BlockSpec((ZC, YC, XC), lambda v: (0, 0, 0))
    packed = pl.BlockSpec((ZC // 4, YC, XC), lambda v: (0, 0, 0))
    chunk_shape = jax.ShapeDtypeStruct((ZC, YC, XC), F32)
    ins = [pl.BlockSpec(memory_space=pltpu.SMEM), view, face, face]
    win = pltpu.VMEM((ZW, YC, XC), F32)
    args = (taps, value, before, after)
    if logs is None:
        return pl.pallas_call(
            functools.partial(first_logs_kernel, g),
            name="first_logs",
            grid=(GROUP,),
            out_shape=chunk_shape,
            in_specs=ins,
            out_specs=chunk,
            scratch_shapes=[win],
            **params(9, 16),
        )(*args)
    return pl.pallas_call(
        functools.partial(last_logs_kernel, g),
        name="last_logs",
        grid=(GROUP,),
        out_shape=(chunk_shape, jax.ShapeDtypeStruct((ZC // 4, YC, XC), F32)),
        in_specs=ins + [chunk, chunk],
        out_specs=(chunk, packed),
        scratch_shapes=[win, pltpu.VMEM((ZC, YC, XC), F32)],
        **params(10, 20),
    )(*args, logs, estimate)


def gather_views(row):
    mine = jnp.arange(VIEWS)[:, None, None] == lax.axis_index(V)
    rows = jnp.where(mine, row[None], 0.0)
    for k in (1, 2, 4):
        rows = rows + lax.ppermute(rows, V, [(i, i ^ k) for i in range(VIEWS)])
    return rows


def add_z(blocks):
    before, after = exchange(blocks[0], blocks[SLABS - 1], "z", 4)
    return jnp.concatenate([before[None], blocks, after[None]], axis=0)


def first_window(slab):
    padded = jnp.pad(slab, ((0, 0), (HALO, HALO), (XC, XC)))
    c = lax.axis_index(V)
    before, own, after = (lax.dynamic_slice_in_dim(padded, XC * (c + k), XC, axis=2) for k in range(3))
    planes = jnp.concatenate([own, pack(before, after)], axis=0)
    me = lax.axis_index(S)

    def rows(k):
        return lax.dynamic_slice_in_dim(planes, YC * k, YW, axis=1)

    got = [rows(me)]
    for k in range(1, SLABS):
        got.append(lax.ppermute(rows(me ^ k), S, [(i, i ^ k) for i in range(SLABS)]))
    got = jnp.stack(got)
    blocks = jnp.stack([lax.dynamic_index_in_dim(got, me ^ k, 0, keepdims=False) for k in range(SLABS)])
    return add_z(blocks)


def next_window(chunk, sides):
    before, after = exchange(sides, sides, V, VIEWS)
    lane = lax.broadcasted_iota(jnp.int32, sides.shape, 2)
    packed = jnp.where(lane < XC // 2, before, after)
    blocks = [chunk.reshape(SLABS, DEPTH, YC, XC), packed.reshape(SLABS, PACKED, YC, XC)]
    blocks = add_z(jnp.concatenate(blocks, axis=1))
    before, after = exchange(blocks[:, :, :HALO], blocks[:, :, YC - HALO :], S, SLABS)
    return jnp.concatenate([before, blocks, after], axis=2)


def matrices_kernel(taps, fy, fx, fp, ax, side, ay):
    v = pl.program_id(0)

    def row_column(rows, columns):
        return tuple(lax.broadcasted_iota(jnp.int32, (rows, columns), d) for d in range(2))

    def stacked(ref, at, value):
        hi, lo = split(value)
        ref[at + (slice(0, XC), slice(0, XC))] = hi
        ref[at + (slice(0, XC), slice(XC, 2 * XC))] = lo
        ref[at + (slice(XC, 2 * XC), slice(0, XC))] = hi
        ref[at + (slice(XC, 2 * XC), slice(XC, 2 * XC))] = jnp.zeros_like(lo)

    def along_y(value):
        hi, lo = split(value)
        column = row_column(*value.shape)[1]
        return jnp.where(column < 2 * YK, hi.astype(F32), lo.astype(F32))

    r, c = row_column(XC, XC)
    stacked(fx, (0,), banded(taps, v, 0, r - c + RADIUS))
    stacked(ax, (0,), banded(taps, v, 0, c - r + RADIUS))
    x_of = jnp.where(r < XC // 2, r % HALO - HALO, r % HALO + XC)
    packed = banded(taps, v, 0, x_of - c + RADIUS)
    for j in range(4):
        stacked(fp, (0, j), jnp.where(r // HALO % 4 == j, packed, 0.0))
    before = banded(taps, v, 0, c - (r % HALO - HALO) + RADIUS)
    after = banded(taps, v, 0, c - (r % HALO + XC) + RADIUS)
    for half in range(2):
        value = jnp.where(r // HALO == GROUP * half + v % GROUP, before, 0.0)
        value = jnp.where(r // HALO == GROUP * (1 - half) + v % GROUP, after, value)
        stacked(side, (0, half), value)
    r, c = row_column(YC, 3 * YK)
    fy[...] = along_y(banded(taps, v, 1, c % YK - HALO - r + RADIUS))
    r, c = row_column(64, 2 * YK)
    hi, lo = split(banded(taps, v, 1, r % 32 - (c % YK - HALO) + RADIUS))
    value = jnp.where(r < 32, hi.astype(F32), jnp.where(c < YK, lo.astype(F32), 0.0))
    ay[0] = value.astype(BF16)


def matrices(taps):
    shapes = [
        (2 * XC, 2 * XC),
        (4, 2 * XC, 2 * XC),
        (2 * XC, 2 * XC),
        (2, 2 * XC, 2 * XC),
        (64, 2 * YK),
    ]
    fy, fx, fp, ax, side, ay = pl.pallas_call(
        matrices_kernel,
        name="matrices",
        grid=(VIEWS,),
        out_shape=[jax.ShapeDtypeStruct((VIEWS * YC, 3 * YK), F32)]
        + [jax.ShapeDtypeStruct((VIEWS,) + shape, BF16) for shape in shapes],
        in_specs=[pl.BlockSpec(memory_space=pltpu.SMEM)],
        out_specs=[pl.BlockSpec((YC, 3 * YK), lambda v: (v, 0))] + [of_view(0, *shape) for shape in shapes],
        **params(1, 16),
    )(taps)
    return (fy, fx, fp), (ax, side), ay


def spread_kernel(got, out):
    for c in range(VIEWS):
        for y in range(SLABS):
            out[:, y * YC : (y + 1) * YC, c * XC : (c + 1) * XC] = got[c, y]


def spread(got):
    planes = 2
    return pl.pallas_call(
        spread_kernel,
        name="spread",
        grid=(DEPTH // planes,),
        out_shape=jax.ShapeDtypeStruct((DEPTH, SLABS * YC, VIEWS * XC), F32),
        in_specs=[pl.BlockSpec((VIEWS, SLABS, planes, YC, XC), lambda b: (0, 0, b, 0, 0))],
        out_specs=pl.BlockSpec((planes, SLABS * YC, VIEWS * XC), lambda b: (b, 0, 0)),
        **params(5, 16),
    )(got)


def per_device(views_data, estimate, kernels):
    everyone = gather_views(kernels[0])
    blocks = views_data[0].reshape(DEPTH, SLABS, YC, VIEWS, XC).transpose(3, 1, 0, 2, 4)
    blocks = blocks.reshape(VIEWS * SLABS, DEPTH, YC, XC)
    blocks, everyone = lax.optimization_barrier((blocks, everyone))
    data = lax.all_to_all(blocks, V + S, 0, 0, tiled=True).reshape(VIEWS, ZC, YC, XC)
    taps = (everyone / jnp.sum(everyone, axis=-1, keepdims=True)).reshape(VIEWS, 3 * TAPS)
    w_forward, w_x, w_y = matrices(taps)
    window = first_window(estimate)
    chunk = window[1 : 1 + SLABS, :DEPTH, HALO : HALO + YC].reshape(ZC, YC, XC)
    groups = range(VIEWS // GROUP)
    for number in range(ITERS):
        if number:
            window = next_window(chunk, sides)
        if not number:
            blurred = [forward(g, taps, window, None, *w_forward) for g in groups]
        faces = []
        for g in groups:
            if number:
                ratio, left, right = forward(g, taps, window, data, *w_forward)
            else:
                ratio, left, right = divide_by(g, data, blurred[g])
            faces.append((ratio,) + exchange(left, right, V, VIEWS))
        edges = []
        for g in groups:
            value, top, bottom = adjoint_x(g, *faces[g], *w_x)
            edges.append((value,) + exchange(top, bottom, S, SLABS))
        ends = []
        for g in groups:
            value, low, high = adjoint_y(g, *edges[g], w_y)
            ends.append((value,) + exchange(low, high, "z", 4))
        logs = adjoint_z(0, taps, *ends[0], None, None)
        chunk, sides = adjoint_z(1, taps, *ends[1], logs, chunk)

    parts = chunk.reshape(1, SLABS, DEPTH, YC, XC)
    parts = jnp.broadcast_to(parts, (VIEWS, SLABS, DEPTH, YC, XC)).reshape(VIEWS * SLABS, DEPTH, YC, XC)
    got = lax.all_to_all(parts, V + S, 0, 0, tiled=True).reshape(VIEWS, SLABS, DEPTH, YC, XC)
    return spread(got)


def solution(mesh):
    fine = Mesh(mesh.devices.reshape(2, 4, 4, 2, 2), V + ("z",) + S)
    gz = ("z",) + S
    return jax.shard_map(
        per_device,
        mesh=fine,
        in_specs=(P(V, gz, None, None), P(gz, None, None), P(V, None, None)),
        out_specs=P(gz, None, None),
        check_vma=False,
    )
```

```python
import functools

import jax
import jax.numpy as jnp
from jax import lax
from jax.experimental import pallas as pl
from jax.experimental.pallas import tpu as pltpu
from jax.sharding import Mesh
from jax.sharding import PartitionSpec as P

TAPS = 31
ITERS = 2
RADIUS = 15
HALO = 16
VIEWS = 8
GROUP = 4
ZC = 64
YC = 24
XC = 128
YW = YC + 2 * HALO
YK = 64
ZW = ZC + 2 * HALO
SLABS = 4
DEPTH = ZC // SLABS
PACKED = DEPTH // 4
V = ("yh", "x")
S = ("yl", "co")
F32 = jnp.float32
BF16 = jnp.bfloat16
MIB = 1024 * 1024


def params(us, mib):
    cost = pl.CostEstimate(flops=int(us * 1e9), bytes_accessed=int(us * 2e6), transcendentals=0)
    return dict(compiler_params=pltpu.CompilerParams(vmem_limit_bytes=mib * MIB), cost_estimate=cost)


def split(value):
    hi = value.astype(BF16)
    return hi, (value - hi.astype(F32)).astype(BF16)


def dot(a, b):
    return jnp.dot(a, b, preferred_element_type=F32)


def banded(taps, v, axis, offsets):
    result = jnp.zeros(offsets.shape, F32)
    for t in range(TAPS):
        result = jnp.where(offsets == t, taps[v, axis * TAPS + t], result)
    return result


def exchange(low, high, axis, size):
    up = [(i, i + 1) for i in range(size - 1)]
    down = [(j, i) for i, j in up]
    return lax.ppermute(high, axis, up), lax.ppermute(low, axis, down)


def z_sum(win, taps, v, flipped, store):
    @pl.loop(0, ZC // 16)
    def _(b):
        z0 = pl.multiple_of(b * 16, 16)
        for y0 in range(0, YC, 8):
            acc = jnp.zeros((16, 8, XC), F32)
            for t in range(TAPS):
                tap = taps[v, 2 * TAPS + (TAPS - 1 - t if flipped else t)]
                acc = acc + tap * win[pl.ds(z0 + t + 1, 16), y0 : y0 + 8, :]
            store(z0, y0, acc)


def blur_planes(g, taps, est, wy, wown, wpack, yown, ypack, win):
    v = pl.program_id(0)

    @pl.when(v == 0)
    def _():
        empty = jnp.zeros((YK - YW, 2 * XC), F32)
        matrix = wy[...].astype(BF16)

        @pl.loop(0, SLABS + 2)
        def _(b):
            for i in range((DEPTH + PACKED) // 2):
                planes = jnp.concatenate([est[b, 2 * i], est[b, 2 * i + 1]], axis=1)
                hi, lo = split(jnp.concatenate([planes, empty], axis=0))
                got = dot(matrix, jnp.concatenate([hi, lo, hi], axis=0))
                if i < DEPTH // 2:
                    dest, first = yown, b * DEPTH * YC + 2 * i * YC
                else:
                    dest, first = ypack, b * PACKED * YC + 2 * (i - DEPTH // 2) * YC
                rows = pl.ds(pl.multiple_of(first, 16), 2 * YC)
                for u in range(GROUP):
                    one = got[u * YC : (u + 1) * YC]
                    hi, lo = split(jnp.concatenate([one[:, :XC], one[:, XC:]], axis=0))
                    dest[u, rows, :] = jnp.concatenate([hi, lo], axis=1)

    step = 12

    @pl.loop(0, ZW // 4 // step)
    def _(b):
        rows = pl.ds(pl.multiple_of(b * step * 4 * YC, 16), step * 4 * YC)
        two = dot(yown[v, rows, :], wown[0])
        own = (two[:, :XC] + two[:, XC:]).reshape(step, 4, YC, XC)
        packed = ypack[v, pl.ds(pl.multiple_of(b * step * YC, 16), step * YC), :]
        for j in range(4):
            two = dot(packed, wpack[0, j])
            out = own[:, j] + (two[:, :XC] + two[:, XC:]).reshape(step, YC, XC)
            for q in range(step):
                win[b * step * 4 + q * 4 + j] = out[q]


def divide(z0, y0, recorded, blurred, ratio, left, right):
    v = pl.program_id(0)
    zs, ys = pl.ds(z0, 16), pl.ds(y0, 8)
    value = recorded[0, zs, ys, :] / blurred
    ratio[0, zs, ys, :] = value
    half = z0 // (ZC // 2)
    slot = lax.broadcasted_iota(jnp.int32, value.shape, 2) // HALO
    zs = pl.ds(z0 - half * (ZC // 2), 16)
    at = GROUP * (1 - half) + v
    first = pltpu.roll(value, HALO * at, 2)
    left[zs, ys, :] = jnp.where(slot == at, first, left[zs, ys, :])
    at = GROUP * half + v
    last = pltpu.roll(value, lax.rem(HALO * at + HALO, XC), 2)
    right[zs, ys, :] = jnp.where(slot == at, last, right[zs, ys, :])


def blur_kernel(g, taps, est, wy, wown, wpack, blurred, yown, ypack, win):
    blur_planes(g, taps, est, wy, wown, wpack, yown, ypack, win)

    def store(z0, y0, value):
        blurred[0, pl.ds(z0, 16), y0 : y0 + 8, :] = value

    z_sum(win, taps, g * GROUP + pl.program_id(0), False, store)


def blur_and_divide_kernel(g, taps, est, wy, wown, wpack, data, ratio, left, right, yown, ypack, win):
    blur_planes(g, taps, est, wy, wown, wpack, yown, ypack, win)

    def store(z0, y0, value):
        divide(z0, y0, data, value, ratio, left, right)

    z_sum(win, taps, g * GROUP + pl.program_id(0), False, store)


def divide_kernel(data, blurred, ratio, left, right):
    @pl.loop(0, ZC // 16)
    def _(b):
        z0 = pl.multiple_of(b * 16, 16)
        for y0 in range(0, YC, 8):
            divide(z0, y0, data, blurred[0, pl.ds(z0, 16), y0 : y0 + 8, :], ratio, left, right)


def of_view(g, *shape):
    return pl.BlockSpec((1,) + shape, lambda v: (v + g * GROUP,) + (0,) * len(shape))


OUT_VIEW = pl.BlockSpec((1, ZC, YC, XC), lambda v: (v, 0, 0, 0))
OUT_SIDES = pl.BlockSpec((ZC // 2, YC, XC), lambda v: (0, 0, 0))
VIEW_SHAPE = jax.ShapeDtypeStruct((GROUP, ZC, YC, XC), F32)
SIDES_SHAPE = jax.ShapeDtypeStruct((ZC // 2, YC, XC), F32)


def forward(g, taps, window, data, wy, wown, wpack):
    ins = [
        pl.BlockSpec(memory_space=pltpu.SMEM),
        pl.BlockSpec(window.shape, lambda v: (0, 0, 0, 0), pipeline_mode=pl.Buffered(1)),
        pl.BlockSpec((GROUP * YC, 3 * YK), lambda v: (g, 0), pipeline_mode=pl.Buffered(1)),
        of_view(g, 2 * XC, 2 * XC),
        of_view(g, 4, 2 * XC, 2 * XC),
    ]
    scratch = [
        pltpu.VMEM((GROUP, ZW * YC, 2 * XC), BF16),
        pltpu.VMEM((GROUP, ZW // 4 * YC, 2 * XC), BF16),
        pltpu.VMEM((ZW, YC, XC), F32),
    ]
    if data is None:
        return pl.pallas_call(
            functools.partial(blur_kernel, g),
            name="blur",
            grid=(GROUP,),
            out_shape=VIEW_SHAPE,
            in_specs=ins,
            out_specs=OUT_VIEW,
            scratch_shapes=scratch,
            **params(18, 32),
        )(taps, window, wy, wown, wpack)
    return pl.pallas_call(
        functools.partial(blur_and_divide_kernel, g),
        name="blur_and_divide",
        grid=(GROUP,),
        out_shape=(VIEW_SHAPE, SIDES_SHAPE, SIDES_SHAPE),
        in_specs=ins + [of_view(g, ZC, YC, XC)],
        out_specs=(OUT_VIEW, OUT_SIDES, OUT_SIDES),
        scratch_shapes=scratch,
        **params(1, 32),
    )(taps, window, wy, wown, wpack, data)


def divide_by(g, data, blurred):
    return pl.pallas_call(
        divide_kernel,
        name="divide",
        grid=(GROUP,),
        out_shape=(VIEW_SHAPE, SIDES_SHAPE, SIDES_SHAPE),
        in_specs=[of_view(g, ZC, YC, XC), OUT_VIEW],
        out_specs=(OUT_VIEW, OUT_SIDES, OUT_SIDES),
        **params(5, 16),
    )(data, blurred)


def adjoint_x_kernel(ratio, before, after, wown, wside, out, top, bottom):
    planes = ZC // 2
    low_lanes = lax.broadcasted_iota(jnp.int32, (planes * YC, XC), 1) < XC // 2

    @pl.loop(0, 2)
    def _(half):
        rows = planes * YC
        zs = pl.ds(pl.multiple_of(half * planes, planes), planes)
        hi, lo = split(ratio[0, zs].reshape(rows, XC))
        is_before = low_lanes == (half == 0)
        shi, slo = split(jnp.where(is_before, before[...].reshape(rows, XC), after[...].reshape(rows, XC)))
        two = dot(jnp.concatenate([hi, lo], axis=1), wown[0])
        two = two + dot(jnp.concatenate([shi, slo], axis=1), wside[0, half])
        value = two[:, :XC] + two[:, XC:]
        value = value.reshape(planes, YC, XC)
        out[0, zs] = value
        top[0, zs] = value[:, :HALO]
        bottom[0, zs] = value[:, YC - HALO :]


def adjoint_x(g, ratio, before, after, wown, wside):
    view = pl.BlockSpec((1, ZC, YC, XC), lambda v: (v, 0, 0, 0))
    pack = pl.BlockSpec((ZC // 2, YC, XC), lambda v: (0, 0, 0))
    edge = pl.BlockSpec((1, ZC, HALO, XC), lambda v: (v, 0, 0, 0))
    edge_shape = jax.ShapeDtypeStruct((GROUP, ZC, HALO, XC), F32)
    return pl.pallas_call(
        adjoint_x_kernel,
        name="adjoint_x",
        grid=(GROUP,),
        out_shape=(jax.ShapeDtypeStruct((GROUP, ZC, YC, XC), F32), edge_shape, edge_shape),
        in_specs=[
            view,
            pack,
            pack,
            pl.BlockSpec((1, 2 * XC, 2 * XC), lambda v: (v + g * GROUP, 0, 0)),
            pl.BlockSpec((1, 2, 2 * XC, 2 * XC), lambda v: (v + g * GROUP, 0, 0, 0)),
        ],
        out_specs=(view, edge, edge),
        **params(1, 20),
    )(ratio, before, after, wown, wside)


def adjoint_y_kernel(value, before, after, wy, out, low, high):
    empty = jnp.zeros((YK - YW, 2 * XC), F32)

    def pair(ref, z):
        return jnp.concatenate([ref[0, z], ref[0, z + 1]], axis=1)

    @pl.loop(0, ZC // 2, unroll=4)
    def _(b):
        z = 2 * b
        rows = jnp.concatenate([pair(before, z), pair(value, z), pair(after, z), empty], axis=0)
        hi, lo = split(rows)
        got = dot(wy[0], jnp.concatenate([hi, lo], axis=0))
        got = got[:YC] + got[32 : 32 + YC]
        out[0, z] = got[:, :XC]
        out[0, z + 1] = got[:, XC:]

    low[0] = out[0, :HALO]
    high[0] = out[0, ZC - HALO :]


def adjoint_y(g, value, before, after, wy):
    view = pl.BlockSpec((1, ZC, YC, XC), lambda v: (v, 0, 0, 0))
    edge = pl.BlockSpec((1, ZC, HALO, XC), lambda v: (v, 0, 0, 0))
    face = pl.BlockSpec((1, HALO, YC, XC), lambda v: (v, 0, 0, 0))
    face_shape = jax.ShapeDtypeStruct((GROUP, HALO, YC, XC), F32)
    return pl.pallas_call(
        adjoint_y_kernel,
        name="adjoint_y",
        grid=(GROUP,),
        out_shape=(jax.ShapeDtypeStruct((GROUP, ZC, YC, XC), F32), face_shape, face_shape),
        in_specs=[view, edge, edge, of_view(g, 64, 2 * YK)],
        out_specs=(view, face, face),
        **params(8, 16),
    )(value, before, after, wy)


def pack_sides(first, last, q):
    group = lax.broadcasted_iota(jnp.int32, first.shape[1:], 1) // HALO
    acc = jnp.zeros(first.shape[1:], F32)
    for j in range(4):
        acc = jnp.where(group == j, pltpu.roll(first[4 * q + j], HALO * j + HALO, 1), acc)
        acc = jnp.where(group == 4 + j, pltpu.roll(last[4 * q + j], XC // 2 + HALO * j, 1), acc)
    return acc


def sides_kernel(first, last, out):
    for q in range(out.shape[0]):
        out[q] = pack_sides(first, last, q)


def pack(first, last):
    return pl.pallas_call(
        sides_kernel,
        name="sides",
        out_shape=jax.ShapeDtypeStruct((first.shape[0] // 4,) + first.shape[1:], F32),
        **params(1, 16),
    )(first, last)


def add_logs(g, taps, value, before, after, win, total):
    win[:HALO] = before[0]
    win[HALO : HALO + ZC] = value[0]
    win[HALO + ZC :] = after[0]

    def store(z0, y0, back):
        total[pl.ds(z0, 16), y0 : y0 + 8, :] += jnp.log(back)

    z_sum(win, taps, g * GROUP + pl.program_id(0), True, store)


def first_logs_kernel(g, taps, value, before, after, total, win):
    @pl.when(pl.program_id(0) == 0)
    def _():
        total[...] = jnp.zeros_like(total)

    add_logs(g, taps, value, before, after, win, total)


def last_logs_kernel(g, taps, value, before, after, logs, estimate, out, sides, win, total):
    @pl.when(pl.program_id(0) == 0)
    def _():
        total[...] = logs[...]

    add_logs(g, taps, value, before, after, win, total)

    @pl.when(pl.program_id(0) == GROUP - 1)
    def _():
        out[...] = estimate[...] * jnp.exp(total[...] / VIEWS)

        @pl.loop(0, ZC // 4)
        def _(q):
            sides[q] = pack_sides(out, out, q)


def adjoint_z(g, taps, value, before, after, logs, estimate):
    view = pl.BlockSpec((1, ZC, YC, XC), lambda v: (v, 0, 0, 0))
    face = pl.BlockSpec((1, HALO, YC, XC), lambda v: (v, 0, 0, 0))
    chunk = pl.BlockSpec((ZC, YC, XC), lambda v: (0, 0, 0))
    packed = pl.BlockSpec((ZC // 4, YC, XC), lambda v: (0, 0, 0))
    chunk_shape = jax.ShapeDtypeStruct((ZC, YC, XC), F32)
    ins = [pl.BlockSpec(memory_space=pltpu.SMEM), view, face, face]
    win = pltpu.VMEM((ZW, YC, XC), F32)
    args = (taps, value, before, after)
    if logs is None:
        return pl.pallas_call(
            functools.partial(first_logs_kernel, g),
            name="first_logs",
            grid=(GROUP,),
            out_shape=chunk_shape,
            in_specs=ins,
            out_specs=chunk,
            scratch_shapes=[win],
            **params(9, 16),
        )(*args)
    return pl.pallas_call(
        functools.partial(last_logs_kernel, g),
        name="last_logs",
        grid=(GROUP,),
        out_shape=(chunk_shape, jax.ShapeDtypeStruct((ZC // 4, YC, XC), F32)),
        in_specs=ins + [chunk, chunk],
        out_specs=(chunk, packed),
        scratch_shapes=[win, pltpu.VMEM((ZC, YC, XC), F32)],
        **params(10, 20),
    )(*args, logs, estimate)


def gather_views(row):
    mine = jnp.arange(VIEWS)[:, None, None] == lax.axis_index(V)
    rows = jnp.where(mine, row[None], 0.0)
    for k in (1, 2, 4):
        rows = rows + lax.ppermute(rows, V, [(i, i ^ k) for i in range(VIEWS)])
    return rows


def add_z(blocks):
    before, after = exchange(blocks[0], blocks[SLABS - 1], "z", 4)
    return jnp.concatenate([before[None], blocks, after[None]], axis=0)


def first_window(slab):
    padded = jnp.pad(slab, ((0, 0), (HALO, HALO), (XC, XC)))
    c = lax.axis_index(V)
    before, own, after = (lax.dynamic_slice_in_dim(padded, XC * (c + k), XC, axis=2) for k in range(3))
    planes = jnp.concatenate([own, pack(before, after)], axis=0)
    me = lax.axis_index(S)

    def rows(k):
        return lax.dynamic_slice_in_dim(planes, YC * k, YW, axis=1)

    got = [rows(me)]
    for k in range(1, SLABS):
        got.append(lax.ppermute(rows(me ^ k), S, [(i, i ^ k) for i in range(SLABS)]))
    got = jnp.stack(got)
    blocks = jnp.stack([lax.dynamic_index_in_dim(got, me ^ k, 0, keepdims=False) for k in range(SLABS)])
    return add_z(blocks)


def next_window(chunk, sides):
    before, after = exchange(sides, sides, V, VIEWS)
    lane = lax.broadcasted_iota(jnp.int32, sides.shape, 2)
    packed = jnp.where(lane < XC // 2, before, after)
    blocks = [chunk.reshape(SLABS, DEPTH, YC, XC), packed.reshape(SLABS, PACKED, YC, XC)]
    blocks = add_z(jnp.concatenate(blocks, axis=1))
    before, after = exchange(blocks[:, :, :HALO], blocks[:, :, YC - HALO :], S, SLABS)
    return jnp.concatenate([before, blocks, after], axis=2)


def matrices_kernel(taps, fy, fx, fp, ax, side, ay):
    v = pl.program_id(0)

    def row_column(rows, columns):
        return tuple(lax.broadcasted_iota(jnp.int32, (rows, columns), d) for d in range(2))

    def stacked(ref, at, value):
        hi, lo = split(value)
        ref[at + (slice(0, XC), slice(0, XC))] = hi
        ref[at + (slice(0, XC), slice(XC, 2 * XC))] = lo
        ref[at + (slice(XC, 2 * XC), slice(0, XC))] = hi
        ref[at + (slice(XC, 2 * XC), slice(XC, 2 * XC))] = jnp.zeros_like(lo)

    def along_y(value):
        hi, lo = split(value)
        column = row_column(*value.shape)[1]
        return jnp.where(column < 2 * YK, hi.astype(F32), lo.astype(F32))

    r, c = row_column(XC, XC)
    stacked(fx, (0,), banded(taps, v, 0, r - c + RADIUS))
    stacked(ax, (0,), banded(taps, v, 0, c - r + RADIUS))
    x_of = jnp.where(r < XC // 2, r % HALO - HALO, r % HALO + XC)
    packed = banded(taps, v, 0, x_of - c + RADIUS)
    for j in range(4):
        stacked(fp, (0, j), jnp.where(r // HALO % 4 == j, packed, 0.0))
    before = banded(taps, v, 0, c - (r % HALO - HALO) + RADIUS)
    after = banded(taps, v, 0, c - (r % HALO + XC) + RADIUS)
    for half in range(2):
        value = jnp.where(r // HALO == GROUP * half + v % GROUP, before, 0.0)
        value = jnp.where(r // HALO == GROUP * (1 - half) + v % GROUP, after, value)
        stacked(side, (0, half), value)
    r, c = row_column(YC, 3 * YK)
    fy[...] = along_y(banded(taps, v, 1, c % YK - HALO - r + RADIUS))
    r, c = row_column(64, 2 * YK)
    hi, lo = split(banded(taps, v, 1, r % 32 - (c % YK - HALO) + RADIUS))
    value = jnp.where(r < 32, hi.astype(F32), jnp.where(c < YK, lo.astype(F32), 0.0))
    ay[0] = value.astype(BF16)


def matrices(taps):
    shapes = [
        (2 * XC, 2 * XC),
        (4, 2 * XC, 2 * XC),
        (2 * XC, 2 * XC),
        (2, 2 * XC, 2 * XC),
        (64, 2 * YK),
    ]
    fy, fx, fp, ax, side, ay = pl.pallas_call(
        matrices_kernel,
        name="matrices",
        grid=(VIEWS,),
        out_shape=[jax.ShapeDtypeStruct((VIEWS * YC, 3 * YK), F32)]
        + [jax.ShapeDtypeStruct((VIEWS,) + shape, BF16) for shape in shapes],
        in_specs=[pl.BlockSpec(memory_space=pltpu.SMEM)],
        out_specs=[pl.BlockSpec((YC, 3 * YK), lambda v: (v, 0))] + [of_view(0, *shape) for shape in shapes],
        **params(1, 16),
    )(taps)
    return (fy, fx, fp), (ax, side), ay


def spread_kernel(got, out):
    for c in range(VIEWS):
        for y in range(SLABS):
            out[:, y * YC : (y + 1) * YC, c * XC : (c + 1) * XC] = got[c, y]


def spread(got):
    planes = 2
    return pl.pallas_call(
        spread_kernel,
        name="spread",
        grid=(DEPTH // planes,),
        out_shape=jax.ShapeDtypeStruct((DEPTH, SLABS * YC, VIEWS * XC), F32),
        in_specs=[pl.BlockSpec((VIEWS, SLABS, planes, YC, XC), lambda b: (0, 0, b, 0, 0))],
        out_specs=pl.BlockSpec((planes, SLABS * YC, VIEWS * XC), lambda b: (b, 0, 0)),
        **params(5, 16),
    )(got)


def per_device(views_data, estimate, kernels):
    everyone = gather_views(kernels[0])
    blocks = views_data[0].reshape(DEPTH, SLABS, YC, VIEWS, XC).transpose(3, 1, 0, 2, 4)
    blocks = blocks.reshape(VIEWS * SLABS, DEPTH, YC, XC)
    blocks, everyone = lax.optimization_barrier((blocks, everyone))
    data = lax.all_to_all(blocks, V + S, 0, 0, tiled=True).reshape(VIEWS, ZC, YC, XC)
    taps = (everyone / jnp.sum(everyone, axis=-1, keepdims=True)).reshape(VIEWS, 3 * TAPS)
    w_forward, w_x, w_y = matrices(taps)
    window = first_window(estimate)
    chunk = window[1 : 1 + SLABS, :DEPTH, HALO : HALO + YC].reshape(ZC, YC, XC)
    groups = range(VIEWS // GROUP)
    for number in range(ITERS):
        if number:
            window = next_window(chunk, sides)
        if not number:
            blurred = [forward(g, taps, window, None, *w_forward) for g in groups]
            data, *blurred = lax.optimization_barrier((data, *blurred))
        edges = []
        if number:
            for g in groups:
                ratio, left, right = forward(g, taps, window, data, *w_forward)
                value, top, bottom = adjoint_x(g, ratio, *exchange(left, right, V, VIEWS), *w_x)
                if g == 0:
                    window, top, bottom = lax.optimization_barrier((window, top, bottom))
                edges.append((value,) + exchange(top, bottom, S, SLABS))
        else:
            divided = [divide_by(g, data, blurred[g]) for g in groups]
            for g in groups:
                ratio, left, right = divided[g]
                if g:
                    left, right, *_ = lax.optimization_barrier((left, right, top, bottom))
                value, top, bottom = adjoint_x(g, ratio, *exchange(left, right, V, VIEWS), *w_x)
                edges.append((value,) + exchange(top, bottom, S, SLABS))
        ends = []
        for g in groups:
            value, low, high = adjoint_y(g, *edges[g], w_y)
            ends.append((value,) + exchange(low, high, "z", 4))
        logs = adjoint_z(0, taps, *ends[0], None, None)
        chunk, sides = adjoint_z(1, taps, *ends[1], logs, chunk)

    parts = chunk.reshape(1, SLABS, DEPTH, YC, XC)
    parts = jnp.broadcast_to(parts, (VIEWS, SLABS, DEPTH, YC, XC)).reshape(VIEWS * SLABS, DEPTH, YC, XC)
    got = lax.all_to_all(parts, V + S, 0, 0, tiled=True).reshape(VIEWS, SLABS, DEPTH, YC, XC)
    return spread(got)


def solution(mesh):
    fine = Mesh(mesh.devices.reshape(2, 4, 4, 2, 2), V + ("z",) + S)
    gz = ("z",) + S
    return jax.shard_map(
        per_device,
        mesh=fine,
        in_specs=(P(V, gz, None, None), P(gz, None, None), P(V, None, None)),
        out_specs=P(gz, None, None),
        check_vma=False,
    )
```

```python
import functools

import jax
import jax.numpy as jnp
from jax import lax
from jax.experimental import pallas as pl
from jax.experimental.pallas import tpu as pltpu
from jax.sharding import Mesh
from jax.sharding import PartitionSpec as P

TAPS = 31
ITERS = 2
RADIUS = 15
HALO = 16
VIEWS = 8
GROUP = 4
ZC = 64
YC = 24
XC = 128
YW = YC + 2 * HALO
YK = 64
ZW = ZC + 2 * HALO
SLABS = 4
DEPTH = ZC // SLABS
PACKED = DEPTH // 4
V = ("yh", "x")
S = ("yl", "co")
F32 = jnp.float32
BF16 = jnp.bfloat16
MIB = 1024 * 1024


def params(us, mib):
    cost = pl.CostEstimate(flops=int(us * 1e9), bytes_accessed=int(us * 2e6), transcendentals=0)
    return dict(compiler_params=pltpu.CompilerParams(vmem_limit_bytes=mib * MIB), cost_estimate=cost)


def split(value):
    hi = value.astype(BF16)
    return hi, (value - hi.astype(F32)).astype(BF16)


def dot(a, b):
    return jnp.dot(a, b, preferred_element_type=F32)


def banded(taps, v, axis, offsets):
    result = jnp.zeros(offsets.shape, F32)
    for t in range(TAPS):
        result = jnp.where(offsets == t, taps[v, axis * TAPS + t], result)
    return result


def exchange(low, high, axis, size):
    up = [(i, i + 1) for i in range(size - 1)]
    down = [(j, i) for i, j in up]
    return lax.ppermute(high, axis, up), lax.ppermute(low, axis, down)


def z_sum(win, taps, v, flipped, store):
    @pl.loop(0, ZC // 16)
    def _(b):
        z0 = pl.multiple_of(b * 16, 16)
        for y0 in range(0, YC, 8):
            acc = jnp.zeros((16, 8, XC), F32)
            for t in range(TAPS):
                tap = taps[v, 2 * TAPS + (TAPS - 1 - t if flipped else t)]
                acc = acc + tap * win[pl.ds(z0 + t + 1, 16), y0 : y0 + 8, :]
            store(z0, y0, acc)


def blur_planes(g, taps, est, wy, wown, wpack, yown, ypack, win):
    v = pl.program_id(0)

    @pl.when(v == 0)
    def _():
        empty = jnp.zeros((YK - YW, 2 * XC), F32)
        matrix = wy[...].astype(BF16)

        @pl.loop(0, SLABS + 2)
        def _(b):
            for i in range((DEPTH + PACKED) // 2):
                planes = jnp.concatenate([est[b, 2 * i], est[b, 2 * i + 1]], axis=1)
                hi, lo = split(jnp.concatenate([planes, empty], axis=0))
                got = dot(matrix, jnp.concatenate([hi, lo, hi], axis=0))
                if i < DEPTH // 2:
                    dest, first = yown, b * DEPTH * YC + 2 * i * YC
                else:
                    dest, first = ypack, b * PACKED * YC + 2 * (i - DEPTH // 2) * YC
                rows = pl.ds(pl.multiple_of(first, 16), 2 * YC)
                for u in range(GROUP):
                    one = got[u * YC : (u + 1) * YC]
                    hi, lo = split(jnp.concatenate([one[:, :XC], one[:, XC:]], axis=0))
                    dest[u, rows, :] = jnp.concatenate([hi, lo], axis=1)

    step = 24

    @pl.loop(0, ZW // 4 // step)
    def _(b):
        rows = pl.ds(pl.multiple_of(b * step * 4 * YC, 16), step * 4 * YC)
        two = dot(yown[v, rows, :], wown[0])
        own = (two[:, :XC] + two[:, XC:]).reshape(step, 4, YC, XC)
        packed = ypack[v, pl.ds(pl.multiple_of(b * step * YC, 16), step * YC), :]
        for j in range(4):
            two = dot(packed, wpack[0, j])
            out = own[:, j] + (two[:, :XC] + two[:, XC:]).reshape(step, YC, XC)
            for q in range(step):
                win[b * step * 4 + q * 4 + j] = out[q]


def divide(z0, y0, recorded, blurred, ratio, left, right):
    v = pl.program_id(0)
    zs, ys = pl.ds(z0, 16), pl.ds(y0, 8)
    value = recorded[0, zs, ys, :] / blurred
    ratio[0, zs, ys, :] = value
    half = z0 // (ZC // 2)
    slot = lax.broadcasted_iota(jnp.int32, value.shape, 2) // HALO
    zs = pl.ds(z0 - half * (ZC // 2), 16)
    at = GROUP * (1 - half) + v
    first = pltpu.roll(value, HALO * at, 2)
    left[zs, ys, :] = jnp.where(slot == at, first, left[zs, ys, :])
    at = GROUP * half + v
    last = pltpu.roll(value, lax.rem(HALO * at + HALO, XC), 2)
    right[zs, ys, :] = jnp.where(slot == at, last, right[zs, ys, :])


def blur_kernel(g, taps, est, wy, wown, wpack, blurred, yown, ypack, win):
    blur_planes(g, taps, est, wy, wown, wpack, yown, ypack, win)

    def store(z0, y0, value):
        blurred[0, pl.ds(z0, 16), y0 : y0 + 8, :] = value

    z_sum(win, taps, g * GROUP + pl.program_id(0), False, store)


def blur_and_divide_kernel(g, taps, est, wy, wown, wpack, data, ratio, left, right, yown, ypack, win):
    blur_planes(g, taps, est, wy, wown, wpack, yown, ypack, win)

    def store(z0, y0, value):
        divide(z0, y0, data, value, ratio, left, right)

    z_sum(win, taps, g * GROUP + pl.program_id(0), False, store)


def divide_kernel(data, blurred, ratio, left, right):
    @pl.loop(0, ZC // 16)
    def _(b):
        z0 = pl.multiple_of(b * 16, 16)
        for y0 in range(0, YC, 8):
            divide(z0, y0, data, blurred[0, pl.ds(z0, 16), y0 : y0 + 8, :], ratio, left, right)


def of_view(g, *shape):
    return pl.BlockSpec((1,) + shape, lambda v: (v + g * GROUP,) + (0,) * len(shape))


OUT_VIEW = pl.BlockSpec((1, ZC, YC, XC), lambda v: (v, 0, 0, 0))
OUT_SIDES = pl.BlockSpec((ZC // 2, YC, XC), lambda v: (0, 0, 0))
VIEW_SHAPE = jax.ShapeDtypeStruct((GROUP, ZC, YC, XC), F32)
SIDES_SHAPE = jax.ShapeDtypeStruct((ZC // 2, YC, XC), F32)


def forward(g, taps, window, data, wy, wown, wpack):
    ins = [
        pl.BlockSpec(memory_space=pltpu.SMEM),
        pl.BlockSpec(window.shape, lambda v: (0, 0, 0, 0), pipeline_mode=pl.Buffered(1)),
        pl.BlockSpec((GROUP * YC, 3 * YK), lambda v: (g, 0), pipeline_mode=pl.Buffered(1)),
        of_view(g, 2 * XC, 2 * XC),
        of_view(g, 4, 2 * XC, 2 * XC),
    ]
    scratch = [
        pltpu.VMEM((GROUP, ZW * YC, 2 * XC), BF16),
        pltpu.VMEM((GROUP, ZW // 4 * YC, 2 * XC), BF16),
        pltpu.VMEM((ZW, YC, XC), F32),
    ]
    if data is None:
        return pl.pallas_call(
            functools.partial(blur_kernel, g),
            name="blur",
            grid=(GROUP,),
            out_shape=VIEW_SHAPE,
            in_specs=ins,
            out_specs=OUT_VIEW,
            scratch_shapes=scratch,
            **params(18, 32),
        )(taps, window, wy, wown, wpack)
    return pl.pallas_call(
        functools.partial(blur_and_divide_kernel, g),
        name="blur_and_divide",
        grid=(GROUP,),
        out_shape=(VIEW_SHAPE, SIDES_SHAPE, SIDES_SHAPE),
        in_specs=ins + [of_view(g, ZC, YC, XC)],
        out_specs=(OUT_VIEW, OUT_SIDES, OUT_SIDES),
        scratch_shapes=scratch,
        **params(24, 32),
    )(taps, window, wy, wown, wpack, data)


def divide_by(g, data, blurred):
    return pl.pallas_call(
        divide_kernel,
        name="divide",
        grid=(GROUP,),
        out_shape=(VIEW_SHAPE, SIDES_SHAPE, SIDES_SHAPE),
        in_specs=[of_view(g, ZC, YC, XC), OUT_VIEW],
        out_specs=(OUT_VIEW, OUT_SIDES, OUT_SIDES),
        **params(5, 16),
    )(data, blurred)


def adjoint_x_kernel(ratio, before, after, wown, wside, out, top, bottom):
    planes = ZC // 2
    low_lanes = lax.broadcasted_iota(jnp.int32, (planes * YC, XC), 1) < XC // 2

    @pl.loop(0, 2)
    def _(half):
        rows = planes * YC
        zs = pl.ds(pl.multiple_of(half * planes, planes), planes)
        hi, lo = split(ratio[0, zs].reshape(rows, XC))
        is_before = low_lanes == (half == 0)
        shi, slo = split(jnp.where(is_before, before[...].reshape(rows, XC), after[...].reshape(rows, XC)))
        two = dot(jnp.concatenate([hi, lo], axis=1), wown[0])
        two = two + dot(jnp.concatenate([shi, slo], axis=1), wside[0, half])
        value = two[:, :XC] + two[:, XC:]
        value = value.reshape(planes, YC, XC)
        out[0, zs] = value
        top[0, zs] = value[:, :HALO]
        bottom[0, zs] = value[:, YC - HALO :]


def adjoint_x(g, ratio, before, after, wown, wside):
    view = pl.BlockSpec((1, ZC, YC, XC), lambda v: (v, 0, 0, 0))
    pack = pl.BlockSpec((ZC // 2, YC, XC), lambda v: (0, 0, 0))
    edge = pl.BlockSpec((1, ZC, HALO, XC), lambda v: (v, 0, 0, 0))
    edge_shape = jax.ShapeDtypeStruct((GROUP, ZC, HALO, XC), F32)
    return pl.pallas_call(
        adjoint_x_kernel,
        name="adjoint_x",
        grid=(GROUP,),
        out_shape=(jax.ShapeDtypeStruct((GROUP, ZC, YC, XC), F32), edge_shape, edge_shape),
        in_specs=[
            view,
            pack,
            pack,
            pl.BlockSpec((1, 2 * XC, 2 * XC), lambda v: (v + g * GROUP, 0, 0)),
            pl.BlockSpec((1, 2, 2 * XC, 2 * XC), lambda v: (v + g * GROUP, 0, 0, 0)),
        ],
        out_specs=(view, edge, edge),
        **params(8, 20),
    )(ratio, before, after, wown, wside)


def adjoint_y_kernel(value, before, after, wy, out, low, high):
    empty = jnp.zeros((YK - YW, 2 * XC), F32)

    def pair(ref, z):
        return jnp.concatenate([ref[0, z], ref[0, z + 1]], axis=1)

    @pl.loop(0, ZC // 2, unroll=8)
    def _(b):
        z = 2 * b
        rows = jnp.concatenate([pair(before, z), pair(value, z), pair(after, z), empty], axis=0)
        hi, lo = split(rows)
        got = dot(wy[0], jnp.concatenate([hi, lo], axis=0))
        got = got[:YC] + got[32 : 32 + YC]
        out[0, z] = got[:, :XC]
        out[0, z + 1] = got[:, XC:]

    low[0] = out[0, :HALO]
    high[0] = out[0, ZC - HALO :]


def adjoint_y(g, value, before, after, wy):
    view = pl.BlockSpec((1, ZC, YC, XC), lambda v: (v, 0, 0, 0))
    edge = pl.BlockSpec((1, ZC, HALO, XC), lambda v: (v, 0, 0, 0))
    face = pl.BlockSpec((1, HALO, YC, XC), lambda v: (v, 0, 0, 0))
    face_shape = jax.ShapeDtypeStruct((GROUP, HALO, YC, XC), F32)
    return pl.pallas_call(
        adjoint_y_kernel,
        name="adjoint_y",
        grid=(GROUP,),
        out_shape=(jax.ShapeDtypeStruct((GROUP, ZC, YC, XC), F32), face_shape, face_shape),
        in_specs=[view, edge, edge, of_view(g, 64, 2 * YK)],
        out_specs=(view, face, face),
        **params(8, 16),
    )(value, before, after, wy)


def pack_sides(first, last, q):
    group = lax.broadcasted_iota(jnp.int32, first.shape[1:], 1) // HALO
    acc = jnp.zeros(first.shape[1:], F32)
    for j in range(4):
        acc = jnp.where(group == j, pltpu.roll(first[4 * q + j], HALO * j + HALO, 1), acc)
        acc = jnp.where(group == 4 + j, pltpu.roll(last[4 * q + j], XC // 2 + HALO * j, 1), acc)
    return acc


def sides_kernel(first, last, out):
    for q in range(out.shape[0]):
        out[q] = pack_sides(first, last, q)


def pack(first, last):
    return pl.pallas_call(
        sides_kernel,
        name="sides",
        out_shape=jax.ShapeDtypeStruct((first.shape[0] // 4,) + first.shape[1:], F32),
        **params(1, 16),
    )(first, last)


def add_logs(g, taps, value, before, after, win, total):
    win[:HALO] = before[0]
    win[HALO : HALO + ZC] = value[0]
    win[HALO + ZC :] = after[0]

    def store(z0, y0, back):
        total[pl.ds(z0, 16), y0 : y0 + 8, :] += jnp.log(back)

    z_sum(win, taps, g * GROUP + pl.program_id(0), True, store)


def first_logs_kernel(g, taps, value, before, after, total, win):
    @pl.when(pl.program_id(0) == 0)
    def _():
        total[...] = jnp.zeros_like(total)

    add_logs(g, taps, value, before, after, win, total)


def last_logs_kernel(g, taps, value, before, after, logs, estimate, out, sides, win, total):
    @pl.when(pl.program_id(0) == 0)
    def _():
        total[...] = logs[...]

    add_logs(g, taps, value, before, after, win, total)

    @pl.when(pl.program_id(0) == GROUP - 1)
    def _():
        out[...] = estimate[...] * jnp.exp(total[...] / VIEWS)

        @pl.loop(0, ZC // 4)
        def _(q):
            sides[q] = pack_sides(out, out, q)


def adjoint_z(g, taps, value, before, after, logs, estimate):
    view = pl.BlockSpec((1, ZC, YC, XC), lambda v: (v, 0, 0, 0))
    face = pl.BlockSpec((1, HALO, YC, XC), lambda v: (v, 0, 0, 0))
    chunk = pl.BlockSpec((ZC, YC, XC), lambda v: (0, 0, 0))
    packed = pl.BlockSpec((ZC // 4, YC, XC), lambda v: (0, 0, 0))
    chunk_shape = jax.ShapeDtypeStruct((ZC, YC, XC), F32)
    ins = [pl.BlockSpec(memory_space=pltpu.SMEM), view, face, face]
    win = pltpu.VMEM((ZW, YC, XC), F32)
    args = (taps, value, before, after)
    if logs is None:
        return pl.pallas_call(
            functools.partial(first_logs_kernel, g),
            name="first_logs",
            grid=(GROUP,),
            out_shape=chunk_shape,
            in_specs=ins,
            out_specs=chunk,
            scratch_shapes=[win],
            **params(9, 16),
        )(*args)
    return pl.pallas_call(
        functools.partial(last_logs_kernel, g),
        name="last_logs",
        grid=(GROUP,),
        out_shape=(chunk_shape, jax.ShapeDtypeStruct((ZC // 4, YC, XC), F32)),
        in_specs=ins + [chunk, chunk],
        out_specs=(chunk, packed),
        scratch_shapes=[win, pltpu.VMEM((ZC, YC, XC), F32)],
        **params(10, 20),
    )(*args, logs, estimate)


def gather_views(row):
    mine = jnp.arange(VIEWS)[:, None, None] == lax.axis_index(V)
    rows = jnp.where(mine, row[None], 0.0)
    for k in (1, 2, 4):
        rows = rows + lax.ppermute(rows, V, [(i, i ^ k) for i in range(VIEWS)])
    return rows


def add_z(blocks):
    before, after = exchange(blocks[0], blocks[SLABS - 1], "z", 4)
    return jnp.concatenate([before[None], blocks, after[None]], axis=0)


def first_window(slab):
    padded = jnp.pad(slab, ((0, 0), (HALO, HALO), (XC, XC)))
    c = lax.axis_index(V)
    before, own, after = (lax.dynamic_slice_in_dim(padded, XC * (c + k), XC, axis=2) for k in range(3))
    planes = jnp.concatenate([own, pack(before, after)], axis=0)
    me = lax.axis_index(S)

    def rows(k):
        return lax.dynamic_slice_in_dim(planes, YC * k, YW, axis=1)

    got = [rows(me)]
    for k in range(1, SLABS):
        got.append(lax.ppermute(rows(me ^ k), S, [(i, i ^ k) for i in range(SLABS)]))
    got = jnp.stack(got)
    blocks = jnp.stack([lax.dynamic_index_in_dim(got, me ^ k, 0, keepdims=False) for k in range(SLABS)])
    return add_z(blocks)


def next_window(chunk, sides):
    before, after = exchange(sides, sides, V, VIEWS)
    lane = lax.broadcasted_iota(jnp.int32, sides.shape, 2)
    packed = jnp.where(lane < XC // 2, before, after)
    blocks = [chunk.reshape(SLABS, DEPTH, YC, XC), packed.reshape(SLABS, PACKED, YC, XC)]
    blocks = add_z(jnp.concatenate(blocks, axis=1))
    before, after = exchange(blocks[:, :, :HALO], blocks[:, :, YC - HALO :], S, SLABS)
    return jnp.concatenate([before, blocks, after], axis=2)


def matrices_kernel(taps, fy, fx, fp, ax, side, ay):
    v = pl.program_id(0)

    def row_column(rows, columns):
        return tuple(lax.broadcasted_iota(jnp.int32, (rows, columns), d) for d in range(2))

    def stacked(ref, at, value):
        hi, lo = split(value)
        ref[at + (slice(0, XC), slice(0, XC))] = hi
        ref[at + (slice(0, XC), slice(XC, 2 * XC))] = lo
        ref[at + (slice(XC, 2 * XC), slice(0, XC))] = hi
        ref[at + (slice(XC, 2 * XC), slice(XC, 2 * XC))] = jnp.zeros_like(lo)

    def along_y(value):
        hi, lo = split(value)
        column = row_column(*value.shape)[1]
        return jnp.where(column < 2 * YK, hi.astype(F32), lo.astype(F32))

    r, c = row_column(XC, XC)
    stacked(fx, (0,), banded(taps, v, 0, r - c + RADIUS))
    stacked(ax, (0,), banded(taps, v, 0, c - r + RADIUS))
    x_of = jnp.where(r < XC // 2, r % HALO - HALO, r % HALO + XC)
    packed = banded(taps, v, 0, x_of - c + RADIUS)
    for j in range(4):
        stacked(fp, (0, j), jnp.where(r // HALO % 4 == j, packed, 0.0))
    before = banded(taps, v, 0, c - (r % HALO - HALO) + RADIUS)
    after = banded(taps, v, 0, c - (r % HALO + XC) + RADIUS)
    for half in range(2):
        value = jnp.where(r // HALO == GROUP * half + v % GROUP, before, 0.0)
        value = jnp.where(r // HALO == GROUP * (1 - half) + v % GROUP, after, value)
        stacked(side, (0, half), value)
    r, c = row_column(YC, 3 * YK)
    fy[...] = along_y(banded(taps, v, 1, c % YK - HALO - r + RADIUS))
    r, c = row_column(64, 2 * YK)
    hi, lo = split(banded(taps, v, 1, r % 32 - (c % YK - HALO) + RADIUS))
    value = jnp.where(r < 32, hi.astype(F32), jnp.where(c < YK, lo.astype(F32), 0.0))
    ay[0] = value.astype(BF16)


def matrices(taps):
    shapes = [
        (2 * XC, 2 * XC),
        (4, 2 * XC, 2 * XC),
        (2 * XC, 2 * XC),
        (2, 2 * XC, 2 * XC),
        (64, 2 * YK),
    ]
    fy, fx, fp, ax, side, ay = pl.pallas_call(
        matrices_kernel,
        name="matrices",
        grid=(VIEWS,),
        out_shape=[jax.ShapeDtypeStruct((VIEWS * YC, 3 * YK), F32)]
        + [jax.ShapeDtypeStruct((VIEWS,) + shape, BF16) for shape in shapes],
        in_specs=[pl.BlockSpec(memory_space=pltpu.SMEM)],
        out_specs=[pl.BlockSpec((YC, 3 * YK), lambda v: (v, 0))] + [of_view(0, *shape) for shape in shapes],
        **params(1, 16),
    )(taps)
    return (fy, fx, fp), (ax, side), ay


def spread_kernel(got, out):
    for c in range(VIEWS):
        for y in range(SLABS):
            out[:, y * YC : (y + 1) * YC, c * XC : (c + 1) * XC] = got[c, y]


def spread(got):
    planes = 2
    return pl.pallas_call(
        spread_kernel,
        name="spread",
        grid=(DEPTH // planes,),
        out_shape=jax.ShapeDtypeStruct((DEPTH, SLABS * YC, VIEWS * XC), F32),
        in_specs=[pl.BlockSpec((VIEWS, SLABS, planes, YC, XC), lambda b: (0, 0, b, 0, 0))],
        out_specs=pl.BlockSpec((planes, SLABS * YC, VIEWS * XC), lambda b: (b, 0, 0)),
        **params(5, 16),
    )(got)


def per_device(views_data, estimate, kernels):
    everyone = gather_views(kernels[0])
    blocks = views_data[0].reshape(DEPTH, SLABS, YC, VIEWS, XC).transpose(3, 1, 0, 2, 4)
    blocks = blocks.reshape(VIEWS * SLABS, DEPTH, YC, XC)
    blocks, everyone = lax.optimization_barrier((blocks, everyone))
    data = lax.all_to_all(blocks, V + S, 0, 0, tiled=True).reshape(VIEWS, ZC, YC, XC)
    taps = (everyone / jnp.sum(everyone, axis=-1, keepdims=True)).reshape(VIEWS, 3 * TAPS)
    w_forward, w_x, w_y = matrices(taps)
    window = first_window(estimate)
    chunk = window[1 : 1 + SLABS, :DEPTH, HALO : HALO + YC].reshape(ZC, YC, XC)
    groups = range(VIEWS // GROUP)
    for number in range(ITERS):
        if number:
            window = next_window(chunk, sides)
        if not number:
            blurred = [forward(g, taps, window, None, *w_forward) for g in groups]
        faces = []
        for g in groups:
            if number:
                ratio, left, right = forward(g, taps, window, data, *w_forward)
            else:
                ratio, left, right = divide_by(g, data, blurred[g])
            faces.append((ratio,) + exchange(left, right, V, VIEWS))
        edges = []
        for g in groups:
            value, top, bottom = adjoint_x(g, *faces[g], *w_x)
            edges.append((value,) + exchange(top, bottom, S, SLABS))
        ends = []
        for g in groups:
            value, low, high = adjoint_y(g, *edges[g], w_y)
            ends.append((value,) + exchange(low, high, "z", 4))
        logs = adjoint_z(0, taps, *ends[0], None, None)
        chunk, sides = adjoint_z(1, taps, *ends[1], logs, chunk)

    parts = chunk.reshape(1, SLABS, DEPTH, YC, XC)
    parts = jnp.broadcast_to(parts, (VIEWS, SLABS, DEPTH, YC, XC)).reshape(VIEWS * SLABS, DEPTH, YC, XC)
    got = lax.all_to_all(parts, V + S, 0, 0, tiled=True).reshape(VIEWS, SLABS, DEPTH, YC, XC)
    return spread(got)


def solution(mesh):
    fine = Mesh(mesh.devices.reshape(2, 4, 4, 2, 2), V + ("z",) + S)
    gz = ("z",) + S
    return jax.shard_map(
        per_device,
        mesh=fine,
        in_specs=(P(V, gz, None, None), P(gz, None, None), P(V, None, None)),
        out_specs=P(gz, None, None),
        check_vma=False,
    )
```
